512 devices in a mesh: pts: 128 (over x, z, core), help: 4 (over y).
Axes of the slice: x: 4, y: 4, z: 16, core: 2. Of those that a mesh axis runs over, the one named last changes fastest.
Arguments:
- src_points: bfloat16 [131072, 256], P(('pts', 'help')), may hold values from -8 to 8
- dst_points: bfloat16 [131072, 256], P(('pts', 'help')), may hold values from -8 to 8
- src_logw: float32 [131072], P(('pts', 'help')), may hold values from -1.2 to 1.2
- dst_logw: float32 [131072], P(('pts', 'help')), may hold values from -1.2 to 1.2
- init_g: float32 [131072], P(('pts', 'help')), may hold values from -2 to 7000
- pair_lists: int32 [512, 24], P(('pts', 'help')), may hold values from 0 to 511, as said below
- pair_counts: int32 [512], P(('pts', 'help')), may hold values from 3 to 24, as said below
Outputs:
- dual_f: float32 [131072], P(('pts', 'help'))
- dual_g: float32 [131072], P(('pts', 'help'))
The draws below stay inside these ranges and needn't reach their ends.
Inputs may be any that keep to these rules, and one draw needn't show every extreme that they name: `pair_lists`: row block r's first pair_counts[r] entries are distinct, one of them is r itself, and each names a block whose points are held by an index of pts at most 3 away from the index that holds r; the later entries equal r. `pair_counts`: 24 is reached by some row block in every draw. The counts of the blocks held by one index of pts sum to at most 14 times the number of help devices; dealt out in turn to the help devices of that index, they give some device exactly 24 in every draw.
All inputs are finite; a program needn't handle non-finite values.
Results may differ from the reference program's by a relative error of at most 0.0003.
Values may be sent and summed in bfloat16 or wider, within the bound.
A program may use at most 64 MiB of HBM per device.

```python
import jax
import jax.numpy as jnp
from jax import lax

D = 256
BLOCK = 256
PAIR_MOST = 24
REACH = 3
ITERS = 2
BLOCKS = 512
POINTS = 131072
N_HELP = 4


def point_cloud(key):
    keys = jax.random.split(jax.random.fold_in(key, 13), 3)
    sources = 0.18 * jnp.clip(jax.random.normal(keys[0], (POINTS, D)), -4.0, 4.0)
    targets = 0.18 * jnp.clip(jax.random.normal(keys[1], (POINTS, D)), -4.0, 4.0)
    jitter = 0.25 * jnp.clip(jax.random.normal(keys[2], (POINTS,)), -3.0, 3.0)
    source_half = sources.astype(jnp.bfloat16)
    target_half = targets.astype(jnp.bfloat16)
    target_wide = target_half.astype(jnp.float32)
    potential = 0.5 * jnp.sum(target_wide * target_wide, axis=1) + jitter
    return (source_half, target_half, potential)


def draw_src_points(key, part):
    return point_cloud(key)[0]


def draw_dst_points(key, part):
    return point_cloud(key)[1]


def draw_init_g(key, part):
    return point_cloud(key)[2]


def pair_tables(key):
    keys = jax.random.split(jax.random.fold_in(key, 29), 7)
    blocks = BLOCKS
    groups = BLOCKS // N_HELP
    owners = jnp.arange(blocks) // N_HELP
    within = jnp.arange(blocks) % N_HELP
    counts = jax.random.randint(keys[0], (blocks,), 3, 11)
    heavy_on = jax.random.randint(keys[1], (groups,), 0, 4) == 0
    heavy_at = jax.random.randint(keys[2], (groups,), 0, N_HELP)
    heavy_count = jax.random.randint(keys[3], (groups,), 16, PAIR_MOST + 1)
    is_heavy = heavy_on[owners] & (heavy_at[owners] == within)
    counts = jnp.where(is_heavy, heavy_count[owners], counts)
    forced = jax.random.randint(keys[4], (), REACH, max(REACH + 1, groups - REACH))
    forced_at = jax.random.randint(keys[5], (), 0, N_HELP)
    counts = jnp.where(owners == forced, jnp.where(within == forced_at, PAIR_MOST, 10), counts)
    lowest = jnp.maximum(owners - REACH, 0)
    highest = jnp.minimum(owners + REACH, groups - 1)
    counts = jnp.minimum(counts, (highest - lowest + 1) * N_HELP)
    spot_count = (2 * REACH + 1) * N_HELP
    slots = jnp.arange(spot_count)
    col_owner = owners[:, None] - REACH + slots[None, :] // N_HELP
    columns = col_owner * N_HELP + slots[None, :] % N_HELP
    usable = (col_owner >= 0) & (col_owner < groups)
    ranking = jax.random.randint(keys[6], (blocks, spot_count), 0, 2 ** 20) * 64 + slots[None, :]
    ranking = jnp.where(usable, ranking, ranking + 2 ** 27)
    ranking = jnp.where(columns == jnp.arange(blocks)[:, None], -1, ranking)
    picked = jnp.argsort(ranking, axis=1, stable=True)[:, :PAIR_MOST]
    chosen = jnp.take_along_axis(columns, picked, axis=1)
    keeping = jnp.arange(PAIR_MOST)[None, :] < counts[:, None]
    chosen = jnp.where(keeping, chosen, jnp.arange(blocks)[:, None])
    return (chosen.astype(jnp.int32), counts.astype(jnp.int32))


def draw_pair_lists(key, part):
    return pair_tables(key)[0]


def draw_pair_counts(key, part):
    return pair_tables(key)[1]


def block_levels(stream_key, extent, cuts, smallest, largest):
    level, own = 1.0, jax.random.fold_in(stream_key, 6)
    for axis_at, shards_of in cuts:
        heights = jnp.exp(jax.random.uniform(jax.random.fold_in(own, axis_at), (shards_of,), jnp.float32, smallest / len(cuts), largest / len(cuts)))
        level = level * jnp.repeat(heights, extent[axis_at] // shards_of).reshape([-1 if axis == axis_at else 1 for axis in range(len(extent))])
    return level


def setup_inputs(seed: int = 0) -> dict:
    key_of = jax.random.split(jax.random.key(seed), 8)
    src_points = draw_src_points(jax.random.fold_in(key_of[7], 71), 0)
    dst_points = draw_dst_points(jax.random.fold_in(key_of[7], 71), 0)
    src_logw = jnp.clip(jax.random.uniform(key_of[2], (POINTS,), jnp.float32, -1.2, 1.2) * block_levels(key_of[2], (POINTS,), ((0, 512),), -0.4, 0.0), -1.2, 1.2)
    dst_logw = jnp.clip(jax.random.uniform(key_of[3], (POINTS,), jnp.float32, -1.2, 1.2) * block_levels(key_of[3], (POINTS,), ((0, 512),), -0.4, 0.0), -1.2, 1.2)
    init_g = draw_init_g(jax.random.fold_in(key_of[7], 71), 0)
    pair_lists = draw_pair_lists(jax.random.fold_in(key_of[7], 71), 0)
    pair_counts = draw_pair_counts(jax.random.fold_in(key_of[7], 71), 0)
    return {"src_points": src_points, "dst_points": dst_points, "src_logw": src_logw, "dst_logw": dst_logw, "init_g": init_g, "pair_lists": pair_lists, "pair_counts": pair_counts}


EPS = 0.25
NEGATIVE = -1.0e30


def reference(src_points, dst_points, src_logw, dst_logw, init_g, pair_lists, pair_counts):
    blocks = pair_lists.shape[0]
    src_full = src_points.astype(jnp.float32).reshape(blocks, BLOCK, D)
    dst_full = dst_points.astype(jnp.float32).reshape(blocks, BLOCK, D)
    src_half = 0.5 * jnp.sum(src_full * src_full, axis=2)
    dst_half = 0.5 * jnp.sum(dst_full * dst_full, axis=2)
    src_weight = src_logw.reshape(blocks, BLOCK)
    dst_weight = dst_logw.reshape(blocks, BLOCK)
    active = jnp.arange(PAIR_MOST, dtype=jnp.int32)[None, :] < pair_counts[:, None]
    dual_g = init_g.reshape(blocks, BLOCK)
    dual_f = jnp.zeros_like(dual_g)
    for sweep_index in range(ITERS):
        def one_block(carry, item):
            col_top, col_sum = carry
            row_pts, row_half, row_weight, columns, active_row = item
            inner_dot = jnp.einsum("nd,kmd->knm", row_pts, dst_full[columns], precision=lax.Precision.HIGHEST)
            cost_tile = row_half[None, :, None] + dst_half[columns][:, None, :] - inner_dot
            scores = dst_weight[columns][:, None, :] + (dual_g[columns][:, None, :] - cost_tile) / EPS
            scores = jnp.where(active_row[:, None, None], scores, NEGATIVE)
            row_top = jnp.max(scores, axis=(0, 2))
            row_sum = jnp.sum(jnp.exp(scores - row_top[None, :, None]), axis=(0, 2))
            block_f = -EPS * (row_top + jnp.log(row_sum))
            col_scores = row_weight[None, :, None] + (block_f[None, :, None] - cost_tile) / EPS
            tile_top = jnp.max(col_scores, axis=1)
            tile_sum = jnp.sum(jnp.exp(col_scores - tile_top[:, None, :]), axis=1)
            tile_top = jnp.where(active_row[:, None], tile_top, NEGATIVE)
            tile_sum = jnp.where(active_row[:, None], tile_sum, 0.0)
            new_top = col_top.at[columns].max(tile_top)
            added = jnp.zeros_like(col_sum).at[columns].add(tile_sum * jnp.exp(tile_top - new_top[columns]))
            new_sum = col_sum * jnp.exp(col_top - new_top) + added
            return (new_top, new_sum), block_f

        initial = (jnp.full((blocks, BLOCK), NEGATIVE, dtype=jnp.float32), jnp.zeros((blocks, BLOCK), dtype=jnp.float32))
        (col_top, col_sum), dual_f = lax.scan(one_block, initial, (src_full, src_half, src_weight, pair_lists, active))
        dual_g = -EPS * (col_top + jnp.log(col_sum))
    return dual_f.reshape(-1), dual_g.reshape(-1)
```

```python
import functools
import math

import jax
import jax.numpy as jnp
from jax import lax
from jax.experimental import pallas as pl
from jax.experimental.pallas import tpu as pltpu
from jax.sharding import PartitionSpec as P

REACH = 3
WIDE = 2 * REACH
SPOTS = 2 * REACH + 1
BLOCK = 256
LOG2E = 1.0 / math.log(2.0)
SCALE = 4.0 * LOG2E
NEG = -1e30
MESH = pl.DeviceIdType.MESH
F32 = jnp.float32


def tree(op, values):
    values = list(values)
    while len(values) > 1:
        paired = [op(a, b) for a, b in zip(values[::2], values[1::2])]
        values = paired + values[len(paired) * 2 :]
    return values[0]


def log2(x):
    return jnp.log(x) * LOG2E


def half_norms(points):
    wide = points.astype(F32)
    square = wide * wide
    high = square.astype(jnp.bfloat16)
    low = (square - high.astype(F32)).astype(jnp.bfloat16)
    ones = jnp.ones((8, points.shape[1]), jnp.bfloat16)
    dims = (((1,), (1,)), ((), ()))
    total = lax.dot_general(ones, high, dims, preferred_element_type=F32)
    total += lax.dot_general(ones, low, dims, preferred_element_type=F32)
    return 0.5 * total


def kernel(
    n_pts,
    n_help,
    src_hbm,
    dst_hbm,
    src_lw,
    dst_lw,
    init_g,
    lists,
    counts,
    out_f,
    out_g,
    xs,
    ys,
    vin,
    yout,
    yin,
    dots,
    peak,
    total,
    bvec,
    acol,
    lsend,
    lrecv,
    gsend,
    grecv,
    glast,
    local_sem,
    xs_send,
    xs_recv,
    ys_send,
    ys_recv,
    vec_send,
    vec_recv,
    row_send,
    row_recv,
    f_send,
    f_recv,
    g_send,
    g_recv,
    e_send,
    e_recv,
):
    p = lax.axis_index("pts")
    h = lax.axis_index("help")
    near = [d for d in range(-REACH, REACH + 1) if d]
    wide = [d for d in range(-WIDE, WIDE + 1) if d]

    def there(d):
        return (p + d >= 0) & (p + d < n_pts)

    def when_there(d, do):
        @pl.when(there(d))
        def _():
            do()

    def helper(j):
        return lax.rem(h + j, n_help)

    def remote(src, dst, send, recv, device):
        return pltpu.make_async_remote_copy(
            src_ref=src,
            dst_ref=dst,
            send_sem=send,
            recv_sem=recv,
            device_id=device,
            device_id_type=MESH,
        )

    for d in near:

        @pl.when(jnp.logical_not(there(d)))
        def _():
            ys[d + REACH] = jnp.zeros(ys.shape[1:], ys.dtype)
            vin[d + REACH] = jnp.zeros(vin.shape[1:], F32)
            glast[d + REACH] = jnp.full(glast.shape[1:], NEG, F32)

    for d in wide:

        @pl.when(jnp.logical_not(there(d)))
        def _():
            for k in range(SPOTS):
                grecv[k, d + WIDE] = jnp.full(grecv.shape[2:], NEG, F32)

    barrier = pltpu.get_barrier_semaphore()
    for j in range(1, n_help):
        pl.semaphore_signal(barrier, inc=1, device_id={"help": helper(j)}, device_id_type=MESH)
    for d in wide:
        when_there(
            d,
            lambda d=d: pl.semaphore_signal(
                barrier, inc=1, device_id={"pts": p + d}, device_id_type=MESH
            ),
        )

    get_dst = pltpu.make_async_copy(dst_hbm, ys.at[REACH], local_sem.at[0])
    get_src = pltpu.make_async_copy(src_hbm, xs.at[h], local_sem.at[1])
    get_dst.start()
    get_src.start()

    lane = lax.broadcasted_iota(jnp.int32, (8, 128), 1)
    sub = lax.broadcasted_iota(jnp.int32, (8, 128), 0)
    listed = lists[...]
    width = listed.shape[1]
    slot = lax.broadcasted_iota(jnp.int32, (8, width), 1)
    spot = lax.broadcasted_iota(jnp.int32, (8, width), 0)
    live = slot < counts[0]
    for c in range(n_help):
        column = (p + spot - REACH) * n_help + c
        hit = jnp.where((listed == column) & live, 1.0, 0.0)
        yout[c, 0:8, :] = jnp.broadcast_to(jnp.max(hit, axis=1, keepdims=True), (8, 128))
        yout[c, 8:16, :] = jnp.broadcast_to(
            jnp.concatenate([src_lw[...] * LOG2E] * 4, axis=0), (8, 128)
        )

    get_dst.wait()
    dst_half = half_norms(ys[REACH])
    vin[REACH, 0:1, :] = dst_lw[0:1, :] * LOG2E + SCALE * (init_g[0:1, :] - dst_half[0:1, 0:128])
    vin[REACH, 1:2, :] = dst_lw[1:2, :] * LOG2E + SCALE * (init_g[1:2, :] - dst_half[0:1, 128:256])
    vin[REACH, 2:4, :] = dst_lw[...] * LOG2E
    get_src.wait()
    src_half = half_norms(xs[h])

    pl.semaphore_wait(
        barrier,
        n_help - 1 + jnp.minimum(p, WIDE) + jnp.minimum(n_pts - 1 - p, WIDE),
    )

    def vec_copy(d):
        return remote(
            vin.at[REACH], vin.at[REACH - d], vec_send.at[d + REACH], vec_recv.at[REACH - d], {"pts": p + d}
        )

    def ys_copy(d):
        return remote(
            ys.at[REACH], ys.at[REACH - d], ys_send.at[d + REACH], ys_recv.at[REACH - d], {"pts": p + d}
        )

    def row_copy(j):
        return remote(
            yout.at[helper(j)], yin.at[h], row_send.at[j], row_recv.at[j], {"help": helper(j)}
        )

    def xs_copy(j):
        return remote(xs.at[h], xs.at[h], xs_send.at[j], xs_recv.at[j], {"help": helper(j)})

    steps = [1, -1, 2, -2, 3, -3]
    for j in range(1, n_help):
        row_copy(j).start()
    for d in steps:
        when_there(d, lambda d=d: vec_copy(d).start())
    for j in range(1, n_help):
        xs_copy(j).start()
    for d in steps:
        when_there(d, lambda d=d: ys_copy(d).start())
    yin[h] = yout[h]

    for j in range(1, n_help):
        xs_copy(j).wait_recv()

    def one_spot(step, carry):
        odd = lax.rem(step, 2)
        away = (step + 1) // 2 * (1 - 2 * odd)
        k = REACH + away

        @pl.when((step > 0) & (p + away >= 0) & (p + away < n_pts))
        def _():
            remote(ys.at[REACH], ys.at[k], ys_send.at[k], ys_recv.at[k], {"pts": p + away}).wait_recv()

        for r in range(n_help):
            inner = lax.dot_general(
                xs[r], ys[k], (((1,), (1,)), ((), ())), preferred_element_type=F32
            )
            inner = inner * SCALE
            dots[k, 2 * r] = inner[0:128]
            dots[k, 2 * r + 1] = inner[128:256]
        return carry

    lax.fori_loop(0, SPOTS, one_spot, 0)

    for j in range(1, n_help):
        row_copy(j).wait_recv()
    for d in steps:
        when_there(d, lambda d=d: vec_copy(-d).wait_recv())
    for k in range(SPOTS):
        bvec[k] = vin[k, 0:2, :]

    diagonal = lane - sub

    def row_sweep():
        def one(rh, carry):
            r = rh // 2
            push = []
            for k in range(SPOTS):
                on = yin[r, k : k + 1, :] > 0.5
                for j in range(2):
                    row = jnp.where(on, bvec[k, j : j + 1, :], NEG)
                    push.append(jnp.broadcast_to(row, (8, 128)))
            found = jnp.zeros((8, 128), F32)
            for g in range(16):
                t = [
                    dots[k, rh, 8 * g : 8 * g + 8, 128 * j : 128 * j + 128] + push[2 * k + j]
                    for k in range(SPOTS)
                    for j in range(2)
                ]
                top = tree(jnp.maximum, t)
                s = tree(jnp.add, [jnp.exp2(v - top) for v in t])
                most = jnp.max(top, axis=1, keepdims=True)
                whole = jnp.sum(s * jnp.exp2(top - most), axis=1, keepdims=True)
                found = jnp.where(diagonal == 8 * g, most + log2(whole), found)
            lsend[pl.ds(rh, 1), :] = jnp.sum(found, axis=0, keepdims=True)
            return carry

        lax.fori_loop(0, 2 * n_help, one, 0)

    def column_sweep():
        def one(rh, carry):
            row = jnp.broadcast_to(acol[pl.ds(rh, 1), :], (8, 128))
            lift = [
                jnp.broadcast_to(
                    jnp.sum(jnp.where(diagonal == 8 * g, row, 0.0), axis=1, keepdims=True),
                    (8, 128),
                )
                for g in range(16)
            ]
            for k in range(SPOTS):
                for j in range(2):
                    u = [
                        dots[k, rh, 8 * g : 8 * g + 8, 128 * j : 128 * j + 128] + lift[g]
                        for g in range(16)
                    ]
                    top = tree(jnp.maximum, u)
                    peak[2 * k + j, rh] = top
                    total[2 * k + j, rh] = tree(jnp.add, [jnp.exp2(v - top) for v in u])
            return carry

        lax.fori_loop(0, 2 * n_help, one, 0)

        def close(k, carry):
            for j in range(2):
                tops = [
                    jnp.where(yin[rh // 2, pl.ds(k, 1), :] > 0.5, peak[2 * k + j, rh], NEG)
                    for rh in range(2 * n_help)
                ]
                top = tree(jnp.maximum, tops)
                most = jnp.max(top, axis=0, keepdims=True)
                s = tree(
                    jnp.add,
                    [total[2 * k + j, rh] * jnp.exp2(tops[rh] - most) for rh in range(2 * n_help)],
                )
                gsend[k, j : j + 1, :] = most + log2(jnp.sum(s, axis=0, keepdims=True))
            return carry

        lax.fori_loop(0, SPOTS, close, 0)

    def fold(parts):
        top = tree(jnp.maximum, parts)
        return top + log2(tree(jnp.add, [jnp.exp2(v - top) for v in parts]))

    def f_copy(it, j):
        return remote(
            lsend.at[it], lrecv.at[it, j], f_send.at[it, j], f_recv.at[it, j], {"help": helper(j)}
        )

    def g_copy(d):
        low, count = max(0, d), SPOTS - abs(d)
        return remote(
            gsend.at[0, pl.ds(low, count)],
            grecv.at[pl.ds(low, count), WIDE - d],
            g_send.at[d + WIDE],
            g_recv.at[WIDE - d],
            {"pts": p + d},
        )

    def e_copy(d):
        return remote(
            gsend.at[1, d + REACH],
            glast.at[REACH - d],
            e_send.at[d + REACH],
            e_recv.at[REACH - d],
            {"pts": p + d},
        )

    lsend_all, gsend_all = lsend, gsend
    for it in range(2):
        lsend, gsend = lsend_all.at[it], gsend_all.at[it]
        row_sweep()
        lsend, gsend = lsend_all, gsend_all
        for j in range(1, n_help):
            f_copy(it, j).start()
        for j in range(1, n_help):
            f_copy(it, j).wait_recv()
        force = -fold([lsend[it]] + [lrecv[it, j] for j in range(1, n_help)])
        for r in range(n_help):
            acol[2 * r : 2 * r + 2, :] = force[2 * r : 2 * r + 2, :] + yin[r, 8:10, :]
        if it == 1:
            lrecv[1, 0] = force
            out_f[0:1, :] = lrecv[1, 0, pl.ds(2 * h, 1), :] * (1.0 / SCALE) + src_half[0:1, 0:128]
            out_f[1:2, :] = (
                lrecv[1, 0, pl.ds(2 * h + 1, 1), :] * (1.0 / SCALE) + src_half[0:1, 128:256]
            )
        lsend, gsend = lsend_all.at[it], gsend_all.at[it]
        column_sweep()
        lsend, gsend = lsend_all, gsend_all
        if it == 0:
            for d in wide:
                when_there(d, lambda d=d: g_copy(d).start())
            for k in range(SPOTS):
                grecv[k, WIDE] = gsend[0, k]
            for d in wide:
                when_there(d, lambda d=d: g_copy(-d).wait_recv())
            for k in range(SPOTS):
                parts = [grecv[REACH - e, k + REACH + e] for e in range(-REACH, REACH + 1)]
                bvec[k] = vin[k, 2:4, :] - fold(parts)
        else:
            for d in near:
                when_there(d, lambda d=d: e_copy(d).start())
            glast[REACH] = gsend[1, REACH]
            for d in near:
                when_there(d, lambda d=d: e_copy(-d).wait_recv())
            pot = -fold([glast[k] for k in range(SPOTS)]) * (1.0 / SCALE)
            out_g[0:1, :] = pot[0:1, :] + dst_half[0:1, 0:128]
            out_g[1:2, :] = pot[1:2, :] + dst_half[0:1, 128:256]

    for j in range(1, n_help):
        row_copy(j).wait_send()
        xs_copy(j).wait_send()
        for it in range(2):
            f_copy(it, j).wait_send()
    for d in near:

        @pl.when(there(d))
        def _(d=d):
            vec_copy(d).wait_send()
            ys_copy(d).wait_send()
            e_copy(d).wait_send()

    for d in wide:
        when_there(d, lambda d=d: g_copy(d).wait_send())


def solution(mesh):
    n_pts, n_help = mesh.shape["pts"], mesh.shape["help"]

    def on_device(src_points, dst_points, src_logw, dst_logw, init_g, pair_lists, pair_counts):
        dim = src_points.shape[1]
        vmem = pl.BlockSpec(memory_space=pltpu.VMEM)
        dma = pltpu.SemaphoreType.DMA
        bf16 = jnp.bfloat16
        out = jax.ShapeDtypeStruct((2, 128), F32)
        f, g = pl.pallas_call(
            functools.partial(kernel, n_pts, n_help),
            out_shape=(out, out),
            in_specs=[
                pl.BlockSpec(memory_space=pl.ANY),
                pl.BlockSpec(memory_space=pl.ANY),
                vmem,
                vmem,
                vmem,
                vmem,
                pl.BlockSpec(memory_space=pltpu.SMEM),
            ],
            out_specs=(vmem, vmem),
            scratch_shapes=[
                pltpu.VMEM((n_help, BLOCK, dim), bf16),
                pltpu.VMEM((SPOTS, BLOCK, dim), bf16),
                pltpu.VMEM((SPOTS, 4, 128), F32),
                pltpu.VMEM((n_help, 16, 128), F32),
                pltpu.VMEM((n_help, 16, 128), F32),
                pltpu.VMEM((SPOTS, 2 * n_help, 128, BLOCK), F32),
                pltpu.VMEM((2 * SPOTS, 2 * n_help, 8, 128), F32),
                pltpu.VMEM((2 * SPOTS, 2 * n_help, 8, 128), F32),
                pltpu.VMEM((SPOTS, 2, 128), F32),
                pltpu.VMEM((2 * n_help, 128), F32),
                pltpu.VMEM((2, 2 * n_help, 128), F32),
                pltpu.VMEM((2, n_help, 2 * n_help, 128), F32),
                pltpu.VMEM((2, SPOTS, 2, 128), F32),
                pltpu.VMEM((SPOTS, 2 * WIDE + 1, 2, 128), F32),
                pltpu.VMEM((SPOTS, 2, 128), F32),
                dma((2,)),
                dma((n_help,)),
                dma((n_help,)),
                dma((SPOTS,)),
                dma((SPOTS,)),
                dma((SPOTS,)),
                dma((SPOTS,)),
                dma((n_help,)),
                dma((n_help,)),
                dma((2, n_help)),
                dma((2, n_help)),
                dma((2 * WIDE + 1,)),
                dma((2 * WIDE + 1,)),
                dma((SPOTS,)),
                dma((SPOTS,)),
            ],
            compiler_params=pltpu.CompilerParams(collective_id=0, has_side_effects=True),
            name="sinkhorn",
        )(
            src_points,
            dst_points,
            src_logw.reshape(2, 128),
            dst_logw.reshape(2, 128),
            init_g.reshape(2, 128),
            pair_lists,
            pair_counts,
        )
        return f.reshape(-1), g.reshape(-1)

    rows = P(("pts", "help"))
    blocks = P(("pts", "help"), None)
    return jax.shard_map(
        on_device,
        mesh=mesh,
        in_specs=(blocks, blocks, rows, rows, rows, blocks, rows),
        out_specs=(rows, rows),
        check_vma=False,
    )
```

```python
import functools
import math

import jax
import jax.numpy as jnp
from jax import lax
from jax.experimental import pallas as pl
from jax.experimental.pallas import tpu as pltpu
from jax.sharding import PartitionSpec as P

REACH = 3
WIDE = 2 * REACH
SPOTS = 2 * REACH + 1
BLOCK = 256
LOG2E = 1.0 / math.log(2.0)
SCALE = 4.0 * LOG2E
NEG = -1e30
MESH = pl.DeviceIdType.MESH
F32 = jnp.float32


def tree(op, values):
    values = list(values)
    while len(values) > 1:
        paired = [op(a, b) for a, b in zip(values[::2], values[1::2])]
        values = paired + values[len(paired) * 2 :]
    return values[0]


def log2(x):
    return jnp.log(x) * LOG2E


def half_norms(points):
    wide = points.astype(F32)
    square = wide * wide
    high = square.astype(jnp.bfloat16)
    low = (square - high.astype(F32)).astype(jnp.bfloat16)
    ones = jnp.ones((8, points.shape[1]), jnp.bfloat16)
    dims = (((1,), (1,)), ((), ()))
    total = lax.dot_general(ones, high, dims, preferred_element_type=F32)
    total += lax.dot_general(ones, low, dims, preferred_element_type=F32)
    return 0.5 * total


def kernel(
    n_pts,
    n_help,
    src_hbm,
    dst_hbm,
    src_lw,
    dst_lw,
    init_g,
    lists,
    counts,
    out_f,
    out_g,
    xs,
    ys,
    vin,
    yout,
    yin,
    dots,
    peak,
    total,
    bvec,
    acol,
    lsend,
    lrecv,
    gsend,
    grecv,
    glast,
    local_sem,
    x_send,
    x_recv,
    x_pass,
    y_send,
    y_recv,
    y_pass,
    y_far,
    vec_send,
    vec_recv,
    row_send,
    row_recv,
    f_send,
    f_recv,
    g_send,
    g_recv,
    e_send,
    e_recv,
):
    p = lax.axis_index("pts")
    h = lax.axis_index("help")
    near = [d for d in range(-REACH, REACH + 1) if d]
    wide = [d for d in range(-WIDE, WIDE + 1) if d]

    def there(d):
        return (p + d >= 0) & (p + d < n_pts)

    def when_there(d, do):
        @pl.when(there(d))
        def _():
            do()

    def helper(j):
        return lax.rem(h + j, n_help)

    def remote(src, dst, send, recv, device):
        return pltpu.make_async_remote_copy(
            src_ref=src,
            dst_ref=dst,
            send_sem=send,
            recv_sem=recv,
            device_id=device,
            device_id_type=MESH,
        )

    side = 1 - 2 * lax.rem(p, 2)

    barrier = pltpu.get_barrier_semaphore()
    for j in range(1, n_help):
        pl.semaphore_signal(barrier, inc=1, device_id={"help": helper(j)}, device_id_type=MESH)
    for d in near:
        when_there(
            d,
            lambda d=d: pl.semaphore_signal(
                barrier, inc=1, device_id={"pts": p + d}, device_id_type=MESH
            ),
        )

    get_dst = pltpu.make_async_copy(dst_hbm, ys.at[REACH], local_sem.at[0])
    get_src = pltpu.make_async_copy(src_hbm, xs.at[h], local_sem.at[1])
    get_dst.start()
    get_src.start()

    with jax.named_scope("barrier"):
        pl.semaphore_wait(
            barrier,
            n_help - 1 + jnp.minimum(p, REACH) + jnp.minimum(n_pts - 1 - p, REACH),
        )

    half = BLOCK // 2
    parts = [pl.ds(0, half), pl.ds(half, half)]

    ahead, behind = {"help": helper(1)}, {"help": helper(n_help - 1)}

    def x_own(way, q):
        return remote(
            src_hbm.at[parts[q]],
            xs.at[h, parts[q]],
            x_send.at[way, q],
            x_recv.at[way, q],
            (ahead, behind)[way],
        )

    def x_on(way):
        r = helper(n_help - 1 if way == 0 else 1)
        here = xs.at[r, parts[way]]
        return remote(here, here, x_pass.at[way], x_recv.at[2, way], (ahead, behind)[way])

    def y_own(way, q):
        d = (2, -2)[way]
        return remote(
            dst_hbm.at[parts[q]],
            ys.at[REACH - d, parts[q]],
            y_send.at[way, q],
            y_recv.at[REACH - d, q],
            {"pts": p + d},
        )

    def y_side():
        return remote(
            dst_hbm, ys.at[REACH - side], y_send.at[2, 0], y_recv.at[REACH - side, 0], {"pts": p + side}
        )

    def y_on(way, q):
        d = (-2, 2)[way]
        k = REACH + d - side
        return remote(
            ys.at[REACH + d, parts[q]],
            ys.at[k, parts[q]],
            y_pass.at[way, q],
            y_recv.at[k, q],
            {"pts": p + side},
        )

    def y_over(q):
        k = REACH + 3 * side
        return remote(
            ys.at[REACH + 2 * side, parts[q]],
            ys.at[k, parts[q]],
            y_far.at[q],
            y_recv.at[k, q],
            {"pts": p - side},
        )

    def y_came(k, q):
        return remote(
            dst_hbm.at[parts[q]], ys.at[k, parts[q]], y_far.at[0], y_recv.at[k, q], {"pts": p + side}
        )

    def x_came(way, q):
        r = helper((n_help - 1, 1, 2)[way])
        return remote(
            src_hbm.at[parts[q]], xs.at[r, parts[q]], x_pass.at[0], x_recv.at[way, q], ahead
        )

    x_own(0, 0).start()
    x_own(1, 1).start()
    when_there(2, lambda: y_own(0, 0).start())
    when_there(-2, lambda: y_own(1, 0).start())
    x_own(0, 1).start()
    x_own(1, 0).start()
    when_there(2, lambda: y_own(0, 1).start())
    when_there(-2, lambda: y_own(1, 1).start())
    y_side().start()

    for d in near:

        @pl.when(jnp.logical_not(there(d)))
        def _():
            ys[d + REACH] = jnp.zeros(ys.shape[1:], ys.dtype)
            vin[d + REACH] = jnp.zeros(vin.shape[1:], F32)
            glast[d + REACH] = jnp.full(glast.shape[1:], NEG, F32)

    for d in wide:

        @pl.when(jnp.logical_not(there(d)))
        def _():
            for k in range(SPOTS):
                grecv[k, d + WIDE] = jnp.full(grecv.shape[2:], NEG, F32)

    lane = lax.broadcasted_iota(jnp.int32, (8, 128), 1)
    sub = lax.broadcasted_iota(jnp.int32, (8, 128), 0)
    listed = lists[...]
    width = listed.shape[1]
    slot = lax.broadcasted_iota(jnp.int32, (8, width), 1)
    spot = lax.broadcasted_iota(jnp.int32, (8, width), 0)
    live = slot < counts[0]
    for c in range(n_help):
        column = (p + spot - REACH) * n_help + c
        hit = jnp.where((listed == column) & live, 1.0, 0.0)
        yout[c, 0:8, :] = jnp.broadcast_to(jnp.max(hit, axis=1, keepdims=True), (8, 128))
        yout[c, 8:16, :] = jnp.broadcast_to(
            jnp.concatenate([src_lw[...] * LOG2E] * 4, axis=0), (8, 128)
        )

    get_dst.wait()
    dst_half = half_norms(ys[REACH])
    vin[REACH, 0:1, :] = dst_lw[0:1, :] * LOG2E + SCALE * (init_g[0:1, :] - dst_half[0:1, 0:128])
    vin[REACH, 1:2, :] = dst_lw[1:2, :] * LOG2E + SCALE * (init_g[1:2, :] - dst_half[0:1, 128:256])
    vin[REACH, 2:4, :] = dst_lw[...] * LOG2E

    def vec_copy(d):
        return remote(
            vin.at[REACH], vin.at[REACH - d], vec_send.at[d + REACH], vec_recv.at[REACH - d], {"pts": p + d}
        )

    def row_copy(j):
        return remote(
            yout.at[helper(j)], yin.at[h], row_send.at[j], row_recv.at[j], {"help": helper(j)}
        )

    steps = [1, -1, 2, -2, 3, -3]
    for j in range(1, n_help):
        row_copy(j).start()
    for d in steps:
        when_there(d, lambda d=d: vec_copy(d).start())
    yin[h] = yout[h]
    get_src.wait()
    src_half = half_norms(xs[h])

    with jax.named_scope("relay"):
        x_came(0, 0).wait_recv()
        x_on(0).start()
        x_came(1, 1).wait_recv()
        x_on(1).start()
        for q in range(2):
            for way, d in enumerate((-2, 2)):

                @pl.when(there(d))
                def _(way=way, d=d, q=q):
                    y_came(REACH + d, q).wait_recv()

                    @pl.when((2 * side == d) & there(-side))
                    def _():
                        y_over(q).start()

                    y_on(way, q).start()

        x_came(0, 1).wait_recv()
        x_came(1, 0).wait_recv()
        remote(dst_hbm, ys.at[REACH + side], y_far.at[0], y_recv.at[REACH + side, 0], {"pts": p + side}).wait_recv()

    def tiles(k, rows):
        for r in rows:
            inner = lax.dot_general(
                xs[r], ys[k], (((1,), (1,)), ((), ())), preferred_element_type=F32
            )
            inner = inner * SCALE
            dots[k, 2 * r] = inner[0:half]
            dots[k, 2 * r + 1] = inner[half:]

    def first(c):
        return lax.select(c < 2, REACH + c * side, REACH + 10 - 4 * c)

    def one_first(c, carry):
        tiles(first(c), [helper(j) for j in (0, 1, 3)])
        return carry

    def one_second(c, carry):
        tiles(first(c), [helper(2)])
        return carry

    def one_third(c, carry):
        d = lax.select(c < 2, side - 2 + 4 * c, -3 * side)
        k = REACH + d

        @pl.when(there(d))
        def _():
            for q in range(2):
                y_came(k, q).wait_recv()

        tiles(k, range(n_help))
        return carry

    with jax.named_scope("tiles1"):
        lax.fori_loop(0, 4, one_first, 0)
    with jax.named_scope("xlast"):
        x_came(2, 0).wait_recv()
        x_came(2, 1).wait_recv()
    with jax.named_scope("tiles2"):
        lax.fori_loop(0, 4, one_second, 0)
    with jax.named_scope("tiles3"):
        lax.fori_loop(0, 3, one_third, 0)

    with jax.named_scope("vec"):
        for j in range(1, n_help):
            row_copy(j).wait_recv()
        for d in steps:
            when_there(d, lambda d=d: vec_copy(-d).wait_recv())
    for k in range(SPOTS):
        bvec[k] = vin[k, 0:2, :]

    diagonal = lane - sub

    def row_sweep():
        def one(rh, carry):
            r = rh // 2
            push = []
            for k in range(SPOTS):
                on = yin[r, k : k + 1, :] > 0.5
                for j in range(2):
                    row = jnp.where(on, bvec[k, j : j + 1, :], NEG)
                    push.append(jnp.broadcast_to(row, (8, 128)))
            found = jnp.zeros((8, 128), F32)
            for g in range(16):
                t = [
                    dots[k, rh, 8 * g : 8 * g + 8, 128 * j : 128 * j + 128] + push[2 * k + j]
                    for k in range(SPOTS)
                    for j in range(2)
                ]
                top = tree(jnp.maximum, t)
                s = tree(jnp.add, [jnp.exp2(v - top) for v in t])
                most = jnp.max(top, axis=1, keepdims=True)
                whole = jnp.sum(s * jnp.exp2(top - most), axis=1, keepdims=True)
                found = jnp.where(diagonal == 8 * g, most + log2(whole), found)
            lsend[pl.ds(rh, 1), :] = jnp.sum(found, axis=0, keepdims=True)
            return carry

        lax.fori_loop(0, 2 * n_help, one, 0)

    def column_sweep():
        def one(rh, carry):
            row = jnp.broadcast_to(acol[pl.ds(rh, 1), :], (8, 128))
            lift = [
                jnp.broadcast_to(
                    jnp.sum(jnp.where(diagonal == 8 * g, row, 0.0), axis=1, keepdims=True),
                    (8, 128),
                )
                for g in range(16)
            ]
            for k in range(SPOTS):
                for j in range(2):
                    u = [
                        dots[k, rh, 8 * g : 8 * g + 8, 128 * j : 128 * j + 128] + lift[g]
                        for g in range(16)
                    ]
                    top = tree(jnp.maximum, u)
                    peak[2 * k + j, rh] = top
                    total[2 * k + j, rh] = tree(jnp.add, [jnp.exp2(v - top) for v in u])
            return carry

        lax.fori_loop(0, 2 * n_help, one, 0)

        def close(k, carry):
            for j in range(2):
                tops = [
                    jnp.where(yin[rh // 2, pl.ds(k, 1), :] > 0.5, peak[2 * k + j, rh], NEG)
                    for rh in range(2 * n_help)
                ]
                top = tree(jnp.maximum, tops)
                most = jnp.max(top, axis=0, keepdims=True)
                s = tree(
                    jnp.add,
                    [total[2 * k + j, rh] * jnp.exp2(tops[rh] - most) for rh in range(2 * n_help)],
                )
                gsend[k, j : j + 1, :] = most + log2(jnp.sum(s, axis=0, keepdims=True))
            return carry

        lax.fori_loop(0, SPOTS, close, 0)

    def fold(parts):
        top = tree(jnp.maximum, parts)
        return top + log2(tree(jnp.add, [jnp.exp2(v - top) for v in parts]))

    def f_copy(it, j):
        return remote(
            lsend.at[it], lrecv.at[it, j], f_send.at[it, j], f_recv.at[it, j], {"help": helper(j)}
        )

    def g_copy(d):
        low, count = max(0, d), SPOTS - abs(d)
        return remote(
            gsend.at[0, pl.ds(low, count)],
            grecv.at[pl.ds(low, count), WIDE - d],
            g_send.at[d + WIDE],
            g_recv.at[WIDE - d],
            {"pts": p + d},
        )

    def e_copy(d):
        return remote(
            gsend.at[1, d + REACH],
            glast.at[REACH - d],
            e_send.at[d + REACH],
            e_recv.at[REACH - d],
            {"pts": p + d},
        )

    lsend_all, gsend_all = lsend, gsend
    for it in range(2):
        lsend, gsend = lsend_all.at[it], gsend_all.at[it]
        with jax.named_scope('rows'):
            row_sweep()
        lsend, gsend = lsend_all, gsend_all
        for j in range(1, n_help):
            f_copy(it, j).start()
        with jax.named_scope('fwait'):
            for j in range(1, n_help):
                f_copy(it, j).wait_recv()
        force = -fold([lsend[it]] + [lrecv[it, j] for j in range(1, n_help)])
        for r in range(n_help):
            acol[2 * r : 2 * r + 2, :] = force[2 * r : 2 * r + 2, :] + yin[r, 8:10, :]
        if it == 1:
            lrecv[1, 0] = force
            out_f[0:1, :] = lrecv[1, 0, pl.ds(2 * h, 1), :] * (1.0 / SCALE) + src_half[0:1, 0:128]
            out_f[1:2, :] = (
                lrecv[1, 0, pl.ds(2 * h + 1, 1), :] * (1.0 / SCALE) + src_half[0:1, 128:256]
            )
        lsend, gsend = lsend_all.at[it], gsend_all.at[it]
        with jax.named_scope('cols'):
            column_sweep()
        lsend, gsend = lsend_all, gsend_all
        if it == 0:
            for d in wide:
                when_there(d, lambda d=d: g_copy(d).start())
            for k in range(SPOTS):
                grecv[k, WIDE] = gsend[0, k]
            with jax.named_scope('gwait'):
                for d in wide:
                    when_there(d, lambda d=d: g_copy(-d).wait_recv())
            for k in range(SPOTS):
                came = [grecv[REACH - e, k + REACH + e] for e in range(-REACH, REACH + 1)]
                bvec[k] = vin[k, 2:4, :] - fold(came)
        else:
            for d in near:
                when_there(d, lambda d=d: e_copy(d).start())
            glast[REACH] = gsend[1, REACH]
            with jax.named_scope('ewait'):
                for d in near:
                    when_there(d, lambda d=d: e_copy(-d).wait_recv())
            pot = -fold([glast[k] for k in range(SPOTS)]) * (1.0 / SCALE)
            out_g[0:1, :] = pot[0:1, :] + dst_half[0:1, 0:128]
            out_g[1:2, :] = pot[1:2, :] + dst_half[0:1, 128:256]

    for j in range(1, n_help):
        row_copy(j).wait_send()
        for it in range(2):
            f_copy(it, j).wait_send()
    for way in range(2):
        x_on(way).wait_send()
        for q in range(2):
            x_own(way, q).wait_send()
    y_side().wait_send()
    for q in range(2):
        for way, d in enumerate((2, -2)):
            when_there(d, lambda way=way, q=q: y_own(way, q).wait_send())
            when_there(-d, lambda way=way, q=q: y_on(way, q).wait_send())
        pl.when(there(2 * side) & there(-side))(lambda q=q: y_over(q).wait_send())
    for d in near:

        @pl.when(there(d))
        def _(d=d):
            vec_copy(d).wait_send()
            e_copy(d).wait_send()

    for d in wide:
        when_there(d, lambda d=d: g_copy(d).wait_send())


def solution(mesh):
    n_pts, n_help = mesh.shape["pts"], mesh.shape["help"]

    def on_device(src_points, dst_points, src_logw, dst_logw, init_g, pair_lists, pair_counts):
        dim = src_points.shape[1]
        vmem = pl.BlockSpec(memory_space=pltpu.VMEM)
        dma = pltpu.SemaphoreType.DMA
        bf16 = jnp.bfloat16
        out = jax.ShapeDtypeStruct((2, 128), F32)
        f, g = pl.pallas_call(
            functools.partial(kernel, n_pts, n_help),
            out_shape=(out, out),
            in_specs=[
                pl.BlockSpec(memory_space=pl.ANY),
                pl.BlockSpec(memory_space=pl.ANY),
                vmem,
                vmem,
                vmem,
                vmem,
                pl.BlockSpec(memory_space=pltpu.SMEM),
            ],
            out_specs=(vmem, vmem),
            scratch_shapes=[
                pltpu.VMEM((n_help, BLOCK, dim), bf16),
                pltpu.VMEM((SPOTS, BLOCK, dim), bf16),
                pltpu.VMEM((SPOTS, 4, 128), F32),
                pltpu.VMEM((n_help, 16, 128), F32),
                pltpu.VMEM((n_help, 16, 128), F32),
                pltpu.VMEM((SPOTS, 2 * n_help, 128, BLOCK), F32),
                pltpu.VMEM((2 * SPOTS, 2 * n_help, 8, 128), F32),
                pltpu.VMEM((2 * SPOTS, 2 * n_help, 8, 128), F32),
                pltpu.VMEM((SPOTS, 2, 128), F32),
                pltpu.VMEM((2 * n_help, 128), F32),
                pltpu.VMEM((2, 2 * n_help, 128), F32),
                pltpu.VMEM((2, n_help, 2 * n_help, 128), F32),
                pltpu.VMEM((2, SPOTS, 2, 128), F32),
                pltpu.VMEM((SPOTS, 2 * WIDE + 1, 2, 128), F32),
                pltpu.VMEM((SPOTS, 2, 128), F32),
                dma((2,)),
                dma((2, 2)),
                dma((3, 2)),
                dma((2,)),
                dma((3, 2)),
                dma((SPOTS, 2)),
                dma((2, 2)),
                dma((2,)),
                dma((SPOTS,)),
                dma((SPOTS,)),
                dma((n_help,)),
                dma((n_help,)),
                dma((2, n_help)),
                dma((2, n_help)),
                dma((2 * WIDE + 1,)),
                dma((2 * WIDE + 1,)),
                dma((SPOTS,)),
                dma((SPOTS,)),
            ],
            compiler_params=pltpu.CompilerParams(collective_id=0, has_side_effects=True),
            name="sinkhorn",
        )(
            src_points,
            dst_points,
            src_logw.reshape(2, 128),
            dst_logw.reshape(2, 128),
            init_g.reshape(2, 128),
            pair_lists,
            pair_counts,
        )
        return f.reshape(-1), g.reshape(-1)

    rows = P(("pts", "help"))
    blocks = P(("pts", "help"), None)
    return jax.shard_map(
        on_device,
        mesh=mesh,
        in_specs=(blocks, blocks, rows, rows, rows, blocks, rows),
        out_specs=(rows, rows),
        check_vma=False,
    )
```

```python
import functools
import math

import jax
import jax.numpy as jnp
from jax import lax
from jax.experimental import pallas as pl
from jax.experimental.pallas import tpu as pltpu
from jax.sharding import PartitionSpec as P

REACH = 3
WIDE = 2 * REACH
SPOTS = 2 * REACH + 1
BLOCK = 256
LOG2E = 1.0 / math.log(2.0)
SCALE = 4.0 * LOG2E
NEG = -1e30
MESH = pl.DeviceIdType.MESH
F32 = jnp.float32


def tree(op, values):
    values = list(values)
    while len(values) > 1:
        paired = [op(a, b) for a, b in zip(values[::2], values[1::2])]
        values = paired + values[len(paired) * 2 :]
    return values[0]


def log2(x):
    return jnp.log(x) * LOG2E


def half_norms(points):
    wide = points.astype(F32)
    square = wide * wide
    high = square.astype(jnp.bfloat16)
    low = (square - high.astype(F32)).astype(jnp.bfloat16)
    ones = jnp.ones((8, points.shape[1]), jnp.bfloat16)
    dims = (((1,), (1,)), ((), ()))
    total = lax.dot_general(ones, high, dims, preferred_element_type=F32)
    total += lax.dot_general(ones, low, dims, preferred_element_type=F32)
    return 0.5 * total


def kernel(
    n_pts,
    n_help,
    src_hbm,
    dst_hbm,
    src_lw_hbm,
    dst_lw_hbm,
    init_g_hbm,
    lists_hbm,
    counts_hbm,
    out,
    src_lw,
    dst_lw,
    init_g,
    lists,
    counts,
    xs,
    ys,
    vin,
    yout,
    yin,
    dots,
    peak,
    total,
    cpeak,
    ctotal,
    push,
    lift,
    bvec,
    flast,
    lsend,
    lrecv,
    gsend,
    grecv,
    glast,
    local_sem,
    x_send,
    x_recv,
    x_pass,
    y_send,
    y_recv,
    y_pass,
    y_far,
    vec_send,
    vec_recv,
    row_send,
    row_recv,
    f_send,
    f_recv,
    g_send,
    g_recv,
    e_send,
    e_recv,
):
    p = lax.axis_index("pts")
    h = lax.axis_index("help")
    near = [d for d in range(-REACH, REACH + 1) if d]
    wide = [d for d in range(-WIDE, WIDE + 1) if d]

    def there(d):
        return (p + d >= 0) & (p + d < n_pts)

    def when_there(d, do):
        @pl.when(there(d))
        def _():
            do()

    def helper(j):
        return lax.rem(h + j, n_help)

    def remote(src, dst, send, recv, device):
        return pltpu.make_async_remote_copy(
            src_ref=src,
            dst_ref=dst,
            send_sem=send,
            recv_sem=recv,
            device_id=device,
            device_id_type=MESH,
        )

    side = 1 - 2 * lax.rem(p, 2)

    barrier = pltpu.get_barrier_semaphore()
    for j in range(1, n_help):
        pl.semaphore_signal(barrier, inc=1, device_id={"help": helper(j)}, device_id_type=MESH)
    for d in near:
        when_there(
            d,
            lambda d=d: pl.semaphore_signal(
                barrier, inc=1, device_id={"pts": p + d}, device_id_type=MESH
            ),
        )

    get_dst = pltpu.make_async_copy(dst_hbm, ys.at[REACH], local_sem.at[0])
    get_src = pltpu.make_async_copy(src_hbm, xs.at[h], local_sem.at[1])
    get_small = [
        pltpu.make_async_copy(a, b, local_sem.at[2 + n])
        for n, (a, b) in enumerate(
            [
                (lists_hbm, lists),
                (counts_hbm, counts),
                (dst_lw_hbm, dst_lw),
                (init_g_hbm, init_g),
                (src_lw_hbm, src_lw),
            ]
        )
    ]
    for get in get_small:
        get.start()
    get_dst.start()
    get_src.start()

    with jax.named_scope("barrier"):
        pl.semaphore_wait(
            barrier,
            n_help - 1 + jnp.minimum(p, REACH) + jnp.minimum(n_pts - 1 - p, REACH),
        )

    half = BLOCK // 2
    parts = [pl.ds(0, half), pl.ds(half, half)]

    ahead, behind = {"help": helper(1)}, {"help": helper(n_help - 1)}

    def x_own(way, q):
        return remote(
            src_hbm.at[parts[q]],
            xs.at[h, parts[q]],
            x_send.at[way, q],
            x_recv.at[way, q],
            (ahead, behind)[way],
        )

    def x_on(way):
        r = helper(n_help - 1 if way == 0 else 1)
        here = xs.at[r, parts[way]]
        return remote(here, here, x_pass.at[way], x_recv.at[2, way], (ahead, behind)[way])

    def y_own(way, q):
        d = (2, -2)[way]
        return remote(
            dst_hbm.at[parts[q]],
            ys.at[REACH - d, parts[q]],
            y_send.at[way, q],
            y_recv.at[REACH - d, q],
            {"pts": p + d},
        )

    def y_side():
        return remote(
            dst_hbm, ys.at[REACH - side], y_send.at[2, 0], y_recv.at[REACH - side, 0], {"pts": p + side}
        )

    def y_on(way, q):
        d = (-2, 2)[way]
        k = REACH + d - side
        return remote(
            ys.at[REACH + d, parts[q]],
            ys.at[k, parts[q]],
            y_pass.at[way, q],
            y_recv.at[k, q],
            {"pts": p + side},
        )

    def y_over(q):
        k = REACH + 3 * side
        return remote(
            ys.at[REACH + 2 * side, parts[q]],
            ys.at[k, parts[q]],
            y_far.at[q],
            y_recv.at[k, q],
            {"pts": p - side},
        )

    def y_came(k, q):
        return remote(
            dst_hbm.at[parts[q]], ys.at[k, parts[q]], y_far.at[0], y_recv.at[k, q], {"pts": p + side}
        )

    def x_came(way, q):
        r = helper((n_help - 1, 1, 2)[way])
        return remote(
            src_hbm.at[parts[q]], xs.at[r, parts[q]], x_pass.at[0], x_recv.at[way, q], ahead
        )

    x_own(0, 0).start()
    x_own(1, 1).start()
    when_there(2, lambda: y_own(0, 0).start())
    when_there(-2, lambda: y_own(1, 0).start())
    x_own(0, 1).start()
    x_own(1, 0).start()
    when_there(2, lambda: y_own(0, 1).start())
    when_there(-2, lambda: y_own(1, 1).start())
    y_side().start()

    for d in near:

        @pl.when(jnp.logical_not(there(d)))
        def _():
            ys[d + REACH] = jnp.zeros(ys.shape[1:], ys.dtype)
            vin[d + REACH] = jnp.zeros(vin.shape[1:], F32)
            glast[d + REACH] = jnp.full(glast.shape[1:], NEG, F32)

    for d in wide:

        @pl.when(jnp.logical_not(there(d)))
        def _():
            for k in range(SPOTS):
                grecv[k, d + WIDE] = jnp.full(grecv.shape[2:], NEG, F32)

    for get in get_small:
        get.wait()
    listed = lists[...]
    width = listed.shape[1]
    slot = lax.broadcasted_iota(jnp.int32, (8, width), 1)
    spot = lax.broadcasted_iota(jnp.int32, (8, width), 0)
    live = slot < counts[0]
    for c in range(n_help):
        column = (p + spot - REACH) * n_help + c
        hit = jnp.where((listed == column) & live, 1.0, 0.0)
        yout[c, 0:8, :] = jnp.broadcast_to(jnp.max(hit, axis=1, keepdims=True), (8, 128))
        yout[c, 8:16, :] = jnp.broadcast_to(
            jnp.concatenate([src_lw[...] * LOG2E] * 4, axis=0), (8, 128)
        )

    get_dst.wait()
    dst_half = half_norms(ys[REACH])
    vin[REACH, 0:1, :] = dst_lw[0:1, :] * LOG2E + SCALE * (init_g[0:1, :] - dst_half[0:1, 0:128])
    vin[REACH, 1:2, :] = dst_lw[1:2, :] * LOG2E + SCALE * (init_g[1:2, :] - dst_half[0:1, 128:256])
    vin[REACH, 2:4, :] = dst_lw[...] * LOG2E

    def vec_copy(d):
        return remote(
            vin.at[REACH], vin.at[REACH - d], vec_send.at[d + REACH], vec_recv.at[REACH - d], {"pts": p + d}
        )

    def row_copy(j):
        return remote(
            yout.at[helper(j)], yin.at[h], row_send.at[j], row_recv.at[j], {"help": helper(j)}
        )

    steps = [1, -1, 2, -2, 3, -3]
    for j in range(1, n_help):
        row_copy(j).start()
    for d in steps:
        when_there(d, lambda d=d: vec_copy(d).start())
    yin[h] = yout[h]
    get_src.wait()
    src_half = half_norms(xs[h])

    with jax.named_scope("relay"):
        x_came(0, 0).wait_recv()
        x_on(0).start()
        x_came(1, 1).wait_recv()
        x_on(1).start()
        for q in range(2):
            for way, d in enumerate((-2, 2)):

                @pl.when(there(d))
                def _(way=way, d=d, q=q):
                    y_came(REACH + d, q).wait_recv()

                    @pl.when((2 * side == d) & there(-side))
                    def _():
                        y_over(q).start()

                    y_on(way, q).start()

        x_came(0, 1).wait_recv()
        x_came(1, 0).wait_recv()
        remote(dst_hbm, ys.at[REACH + side], y_far.at[0], y_recv.at[REACH + side, 0], {"pts": p + side}).wait_recv()

    def tiles(k, rows):
        for r in rows:
            inner = lax.dot_general(
                xs[r], ys[k], (((1,), (1,)), ((), ())), preferred_element_type=F32
            )
            inner = inner * SCALE
            for j in range(2):
                for q in range(2):
                    dots[2 * k + j, 2 * r + q] = inner[half * q : half * q + half, 128 * j : 128 * j + 128]

    soon = [h, helper(1), helper(n_help - 1)]

    def one_first(c, carry):
        tiles(lax.select(c < 2, REACH + c * side, REACH + 10 - 4 * c), soon)
        return carry

    def one_later(c, carry):
        d = lax.select(c < 2, side - 2 + 4 * c, -3 * side)
        k = REACH + d

        @pl.when(there(d))
        def _():
            for q in range(2):
                y_came(k, q).wait_recv()

        tiles(k, soon)
        return carry

    with jax.named_scope("tiles1"):
        lax.fori_loop(0, 4, one_first, 0)
    with jax.named_scope("tiles2"):
        lax.fori_loop(0, 3, one_later, 0)
    with jax.named_scope("xlast"):
        x_came(2, 0).wait_recv()
        x_came(2, 1).wait_recv()
    with jax.named_scope("tiles3"):
        for k in range(SPOTS):
            tiles(k, [helper(2)])

    with jax.named_scope("vec"):
        for j in range(1, n_help):
            row_copy(j).wait_recv()
        for d in steps:
            when_there(d, lambda d=d: vec_copy(-d).wait_recv())
    for k in range(SPOTS):
        bvec[k] = vin[k, 0:2, :]

    def fold(parts):
        top = tree(jnp.maximum, parts)
        return top + log2(tree(jnp.add, [jnp.exp2(v - top) for v in parts]))

    def f_copy(it, j, r):
        return remote(
            lsend.at[it, r],
            lrecv.at[it, j, r],
            f_send.at[it, j, r],
            f_recv.at[it, j, r],
            {"help": helper(j)},
        )

    lanes = 2 * SPOTS

    def row_sweep(it):
        def mask(r, carry):
            for k in range(SPOTS):
                on = yin[r, k : k + 1, :] > 0.5
                for j in range(2):
                    push[r, 2 * k + j : 2 * k + j + 1, :] = jnp.where(on, bvec[k, j : j + 1, :], NEG)
            return carry

        lax.fori_loop(0, n_help, mask, 0)

        def load(r, n):
            t = [
                dots[c, 2 * r + n // 16, 8 * (n % 16) : 8 * (n % 16) + 8, :]
                + jnp.broadcast_to(push[r, c : c + 1, :], (8, 128))
                for c in range(lanes)
            ]
            return t, tree(jnp.maximum, t)

        def close(r):
            for q in range(2):
                top = peak[2 * r + q].T
                most = jnp.max(top, axis=0, keepdims=True)
                s = total[2 * r + q].T * jnp.exp2(top - most)
                lsend[it, r, q : q + 1, :] = most + log2(jnp.sum(s, axis=0, keepdims=True))

        def send(r):
            for j in range(1, n_help):
                f_copy(it, j, r).start()

        def one(r, carry):
            before = jnp.maximum(r - 1, 0)
            close(before)
            t, top = load(r, 0)
            for n in range(32):
                later = load(r, n + 1) if n < 31 else None
                at = slice(8 * (n % 16), 8 * (n % 16) + 8)
                peak[2 * r + n // 16, at, :] = top
                total[2 * r + n // 16, at, :] = tree(jnp.add, [jnp.exp2(v - top) for v in t])
                if later:
                    t, top = later

            @pl.when(r > 0)
            def _():
                send(before)

            return carry

        with jax.named_scope("rmain"):
            lax.fori_loop(0, n_help, one, 0)
        with jax.named_scope("rclose"):
            close(n_help - 1)
        send(n_help - 1)

    def column_sweep(it):
        def load(r, n):
            q, c = n // lanes, n % lanes
            u = [
                dots[c, 2 * r + q, 8 * g : 8 * g + 8, :] + lift[q, 8 * g : 8 * g + 8, :]
                for g in range(16)
            ]
            return u, tree(jnp.maximum, u)

        def one(r, carry):
            for j in range(1, n_help):
                f_copy(it, j, r).wait_recv()
            force = -fold([lsend[it, r]] + [lrecv[it, j, r] for j in range(1, n_help)])
            if it == 1:
                flast[r] = force
            force = force + yin[r, 8:10, :]
            for q in range(2):
                lift[q] = jnp.broadcast_to(force[q : q + 1, :], (128, 128)).T
            u, top = load(r, 0)
            for n in range(2 * lanes):
                later = load(r, n + 1) if n + 1 < 2 * lanes else None
                q, c = n // lanes, n % lanes
                cpeak[c, 2 * r + q] = top
                ctotal[c, 2 * r + q] = tree(jnp.add, [jnp.exp2(v - top) for v in u])
                if later:
                    u, top = later
            return carry

        with jax.named_scope("cmain"):
            lax.fori_loop(0, n_help, one, 0)

        def close(k):
            for j in range(2):
                tops = [
                    jnp.where(yin[rh // 2, k : k + 1, :] > 0.5, cpeak[2 * k + j, rh], NEG)
                    for rh in range(2 * n_help)
                ]
                top = tree(jnp.maximum, tops)
                most = jnp.max(top, axis=0, keepdims=True)
                s = tree(
                    jnp.add,
                    [ctotal[2 * k + j, rh] * jnp.exp2(tops[rh] - most) for rh in range(2 * n_help)],
                )
                gsend[it, k, j : j + 1, :] = most + log2(jnp.sum(s, axis=0, keepdims=True))

        with jax.named_scope("cclose"):
            for k in range(SPOTS):
                close(k)

    def g_copy(d):
        low, count = max(0, d), SPOTS - abs(d)
        return remote(
            gsend.at[0, pl.ds(low, count)],
            grecv.at[pl.ds(low, count), WIDE - d],
            g_send.at[d + WIDE],
            g_recv.at[WIDE - d],
            {"pts": p + d},
        )

    def e_copy(d):
        return remote(
            gsend.at[1, d + REACH],
            glast.at[REACH - d],
            e_send.at[d + REACH],
            e_recv.at[REACH - d],
            {"pts": p + d},
        )

    for it in range(2):
        with jax.named_scope('rows'):
            row_sweep(it)
        with jax.named_scope('cols'):
            column_sweep(it)
        if it == 1:
            pot = flast[h] * (1.0 / SCALE)
            out[0:1, :] = pot[0:1, :] + src_half[0:1, 0:128]
            out[1:2, :] = pot[1:2, :] + src_half[0:1, 128:256]
        if it == 0:
            for d in wide:
                when_there(d, lambda d=d: g_copy(d).start())
            for k in range(SPOTS):
                grecv[k, WIDE] = gsend[0, k]
            with jax.named_scope('gwait'):
                for d in wide:
                    when_there(d, lambda d=d: g_copy(-d).wait_recv())
            for k in range(SPOTS):
                came = [grecv[REACH - e, k + REACH + e] for e in range(-REACH, REACH + 1)]
                bvec[k] = vin[k, 2:4, :] - fold(came)
        else:
            for d in near:
                when_there(d, lambda d=d: e_copy(d).start())
            glast[REACH] = gsend[1, REACH]
            with jax.named_scope('ewait'):
                for d in near:
                    when_there(d, lambda d=d: e_copy(-d).wait_recv())
            pot = -fold([glast[k] for k in range(SPOTS)]) * (1.0 / SCALE)
            out[2:3, :] = pot[0:1, :] + dst_half[0:1, 0:128]
            out[3:4, :] = pot[1:2, :] + dst_half[0:1, 128:256]

    for j in range(1, n_help):
        row_copy(j).wait_send()
        for it in range(2):
            for r in range(n_help):
                f_copy(it, j, r).wait_send()
    for way in range(2):
        x_on(way).wait_send()
        for q in range(2):
            x_own(way, q).wait_send()
    y_side().wait_send()
    for q in range(2):
        for way, d in enumerate((2, -2)):
            when_there(d, lambda way=way, q=q: y_own(way, q).wait_send())
            when_there(-d, lambda way=way, q=q: y_on(way, q).wait_send())
        pl.when(there(2 * side) & there(-side))(lambda q=q: y_over(q).wait_send())
    for d in near:

        @pl.when(there(d))
        def _(d=d):
            vec_copy(d).wait_send()
            e_copy(d).wait_send()

    for d in wide:
        when_there(d, lambda d=d: g_copy(d).wait_send())


def solution(mesh):
    n_pts, n_help = mesh.shape["pts"], mesh.shape["help"]

    def on_device(src_points, dst_points, src_logw, dst_logw, init_g, pair_lists, pair_counts):
        dim = src_points.shape[1]
        vmem = pl.BlockSpec(memory_space=pltpu.VMEM)
        dma = pltpu.SemaphoreType.DMA
        bf16 = jnp.bfloat16
        raw = pl.pallas_call(
            functools.partial(kernel, n_pts, n_help),
            out_shape=jax.ShapeDtypeStruct((4, 128), F32),
            in_specs=[
                pl.BlockSpec(memory_space=pltpu.HBM),
            ]
            * 7,
            out_specs=vmem,
            scratch_shapes=[
                pltpu.VMEM((2, 128), F32),
                pltpu.VMEM((2, 128), F32),
                pltpu.VMEM((2, 128), F32),
                pltpu.VMEM(pair_lists.shape, jnp.int32),
                pltpu.SMEM((1,), jnp.int32),
                pltpu.VMEM((n_help, BLOCK, dim), bf16),
                pltpu.VMEM((SPOTS, BLOCK, dim), bf16),
                pltpu.VMEM((SPOTS, 4, 128), F32),
                pltpu.VMEM((n_help, 16, 128), F32),
                pltpu.VMEM((n_help, 16, 128), F32),
                pltpu.VMEM((2 * SPOTS, 2 * n_help, 128, 128), F32),
                pltpu.VMEM((2 * n_help, 128, 128), F32),
                pltpu.VMEM((2 * n_help, 128, 128), F32),
                pltpu.VMEM((2 * SPOTS, 2 * n_help, 8, 128), F32),
                pltpu.VMEM((2 * SPOTS, 2 * n_help, 8, 128), F32),
                pltpu.VMEM((n_help, 2 * SPOTS, 128), F32),
                pltpu.VMEM((2, 128, 128), F32),
                pltpu.VMEM((SPOTS, 2, 128), F32),
                pltpu.VMEM((n_help, 2, 128), F32),
                pltpu.VMEM((2, n_help, 2, 128), F32),
                pltpu.VMEM((2, n_help, n_help, 2, 128), F32),
                pltpu.VMEM((2, SPOTS, 2, 128), F32),
                pltpu.VMEM((SPOTS, 2 * WIDE + 1, 2, 128), F32),
                pltpu.VMEM((SPOTS, 2, 128), F32),
                dma((7,)),
                dma((2, 2)),
                dma((3, 2)),
                dma((2,)),
                dma((3, 2)),
                dma((SPOTS, 2)),
                dma((2, 2)),
                dma((2,)),
                dma((SPOTS,)),
                dma((SPOTS,)),
                dma((n_help,)),
                dma((n_help,)),
                dma((2, n_help, n_help)),
                dma((2, n_help, n_help)),
                dma((2 * WIDE + 1,)),
                dma((2 * WIDE + 1,)),
                dma((SPOTS,)),
                dma((SPOTS,)),
            ],
            compiler_params=pltpu.CompilerParams(collective_id=0, has_side_effects=True, vmem_limit_bytes=24 << 20),
            name="sinkhorn",
        )(
            *(pltpu.with_memory_space_constraint(v, pltpu.HBM) for v in (src_points, dst_points, src_logw.reshape(2, 128), dst_logw.reshape(2, 128), init_g.reshape(2, 128), pair_lists)), pair_counts,
        )
        return raw[0:2].reshape(-1), raw[2:4].reshape(-1)

    rows = P(("pts", "help"))
    blocks = P(("pts", "help"), None)
    return jax.shard_map(
        on_device,
        mesh=mesh,
        in_specs=(blocks, blocks, rows, rows, rows, blocks, rows),
        out_specs=(rows, rows),
        check_vma=False,
    )
```

```python
import functools
import math

import jax
import jax.numpy as jnp
from jax import lax
from jax.experimental import pallas as pl
from jax.experimental.pallas import tpu as pltpu
from jax.sharding import PartitionSpec as P

REACH = 3
WIDE = 2 * REACH
SPOTS = 2 * REACH + 1
BLOCK = 256
LOG2E = 1.0 / math.log(2.0)
SCALE = 4.0 * LOG2E
NEG = -1e30
FROM_VMEM = True
SEND_AT = 8
MESH = pl.DeviceIdType.MESH
F32 = jnp.float32


def tree(op, values):
    values = list(values)
    while len(values) > 1:
        paired = [op(a, b) for a, b in zip(values[::2], values[1::2])]
        values = paired + values[len(paired) * 2 :]
    return values[0]


def log2(x):
    return jnp.log(x) * LOG2E


def half_norms(points):
    wide = points.astype(F32)
    square = wide * wide
    high = square.astype(jnp.bfloat16)
    low = (square - high.astype(F32)).astype(jnp.bfloat16)
    ones = jnp.ones((8, points.shape[1]), jnp.bfloat16)
    dims = (((1,), (1,)), ((), ()))
    total = lax.dot_general(ones, high, dims, preferred_element_type=F32)
    total += lax.dot_general(ones, low, dims, preferred_element_type=F32)
    return 0.5 * total


def kernel(
    n_pts,
    n_help,
    src_hbm,
    dst_hbm,
    src_lw_hbm,
    dst_lw_hbm,
    init_g_hbm,
    lists_hbm,
    counts_hbm,
    out,
    vals,
    lists,
    counts,
    xs,
    ys,
    vin,
    yout,
    yin,
    dots,
    peak,
    total,
    cpeak,
    ctotal,
    push,
    lift,
    bvec,
    flast,
    lsend,
    lrecv,
    gsend,
    grecv,
    glast,
    local_sem,
    sent,
    x_recv,
    y_recv,
    f_recv,
    g_recv,
    came,
):
    p = lax.axis_index("pts")
    h = lax.axis_index("help")
    near = [d for d in range(-REACH, REACH + 1) if d]
    wide = [d for d in range(-WIDE, WIDE + 1) if d]

    def there(d):
        return (p + d >= 0) & (p + d < n_pts)

    def when_there(d, do):
        @pl.when(there(d))
        def _():
            do()

    def helper(j):
        return lax.rem(h + j, n_help)

    def remote(src, dst, send, recv, device):
        return pltpu.make_async_remote_copy(
            src_ref=src,
            dst_ref=dst,
            send_sem=send,
            recv_sem=recv,
            device_id=device,
            device_id_type=MESH,
        )

    side = 1 - 2 * lax.rem(p, 2)

    barrier = pltpu.get_barrier_semaphore()
    for j in range(1, n_help):
        pl.semaphore_signal(barrier, inc=1, device_id={"help": helper(j)}, device_id_type=MESH)
    for d in near:
        when_there(
            d,
            lambda d=d: pl.semaphore_signal(
                barrier, inc=1, device_id={"pts": p + d}, device_id_type=MESH
            ),
        )

    get_dst = pltpu.make_async_copy(dst_hbm, ys.at[REACH], local_sem.at[0])
    get_src = pltpu.make_async_copy(src_hbm, xs.at[h], local_sem.at[4])
    get_vals = [
        pltpu.make_async_copy(a, vals.at[n], local_sem.at[3])
        for n, a in enumerate([dst_lw_hbm, init_g_hbm, src_lw_hbm])
    ]
    get_lists = pltpu.make_async_copy(lists_hbm, lists, local_sem.at[1])
    get_counts = pltpu.make_async_copy(counts_hbm, counts, local_sem.at[2])
    for get in [get_dst, get_src, get_lists, get_counts, *get_vals]:
        get.start()

    with jax.named_scope("barrier"):
        pl.semaphore_wait(
            barrier,
            n_help - 1 + jnp.minimum(p, REACH) + jnp.minimum(n_pts - 1 - p, REACH),
        )

    half = BLOCK // 2
    parts = [pl.ds(0, half), pl.ds(half, half)]

    ahead, behind = {"help": helper(1)}, {"help": helper(n_help - 1)}

    own_x, own_y = (xs.at[h], ys.at[REACH]) if FROM_VMEM else (src_hbm, dst_hbm)

    def x_own(way, q):
        return remote(
            own_x.at[parts[q]],
            xs.at[h, parts[q]],
            sent.at[0],
            x_recv.at[way if q == way else 2],
            (ahead, behind)[way],
        )

    def x_on(way):
        r = helper(n_help - 1 if way == 0 else 1)
        here = xs.at[r, parts[way]]
        return remote(here, here, sent.at[0], x_recv.at[3], (ahead, behind)[way])

    def y_own(way, q):
        d = (2, -2)[way]
        return remote(
            own_y.at[parts[q]],
            ys.at[REACH - d, parts[q]],
            sent.at[1],
            y_recv.at[2 * way + q],
            {"pts": p + d},
        )

    def y_side():
        return remote(own_y, ys.at[REACH - side], sent.at[1], y_recv.at[4], {"pts": p + side})

    def y_on(way, q):
        d = (-2, 2)[way]
        return remote(
            ys.at[REACH + d, parts[q]],
            ys.at[REACH + d - side, parts[q]],
            sent.at[1],
            y_recv.at[5 + way],
            {"pts": p + side},
        )

    def y_over(q):
        return remote(
            ys.at[REACH + 2 * side, parts[q]],
            ys.at[REACH + 3 * side, parts[q]],
            sent.at[1],
            y_recv.at[7],
            {"pts": p - side},
        )

    def arrive(ref, sem):
        remote(ref, ref, sent.at[0], sem, ahead).wait_recv()

    def leave(ref, sem):
        remote(ref, ref, sem, x_recv.at[0], ahead).wait_send()

    def by_count(count, most, do):
        for c in range(1, most + 1):
            pl.when(count == c)(lambda c=c: do(c))

    lefts, rights = jnp.minimum(p, WIDE), jnp.minimum(n_pts - 1 - p, WIDE)
    nears = jnp.minimum(p, REACH) + jnp.minimum(n_pts - 1 - p, REACH)

    if FROM_VMEM:
        get_dst.wait()
        get_src.wait()
    x_own(0, 0).start()
    x_own(1, 1).start()
    when_there(2, lambda: y_own(0, 0).start())
    when_there(-2, lambda: y_own(1, 0).start())
    x_own(0, 1).start()
    x_own(1, 0).start()
    when_there(2, lambda: y_own(0, 1).start())
    when_there(-2, lambda: y_own(1, 1).start())
    y_side().start()

    for d in near:

        @pl.when(jnp.logical_not(there(d)))
        def _():
            ys[d + REACH] = jnp.zeros(ys.shape[1:], ys.dtype)
            vin[d + REACH] = jnp.zeros(vin.shape[1:], F32)
            glast[d + REACH] = jnp.full(glast.shape[1:], NEG, F32)

    for d in wide:

        @pl.when(jnp.logical_not(there(d)))
        def _():
            grecv[d + WIDE] = jnp.full(grecv.shape[1:], NEG, F32)

    for get in [get_lists, get_counts]:
        get.wait()
    remote(vals, vals, local_sem.at[3], x_recv.at[0], ahead).wait_send()
    dst_lw, init_g, src_lw = vals.at[0], vals.at[1], vals.at[2]
    listed = lists[...]
    width = listed.shape[1]
    slot = lax.broadcasted_iota(jnp.int32, (8, width), 1)
    spot = lax.broadcasted_iota(jnp.int32, (8, width), 0)
    live = slot < counts[0]
    for c in range(n_help):
        column = (p + spot - REACH) * n_help + c
        hit = jnp.where((listed == column) & live, 1.0, 0.0)
        yout[c, 0:8, :] = jnp.broadcast_to(jnp.max(hit, axis=1, keepdims=True), (8, 128))
        yout[c, 8:16, :] = jnp.broadcast_to(
            jnp.concatenate([src_lw[...] * LOG2E] * 4, axis=0), (8, 128)
        )

    if not FROM_VMEM:
        get_dst.wait()
    dst_half = half_norms(ys[REACH])
    vin[REACH, 0:1, :] = dst_lw[0:1, :] * LOG2E + SCALE * (init_g[0:1, :] - dst_half[0:1, 0:128])
    vin[REACH, 1:2, :] = dst_lw[1:2, :] * LOG2E + SCALE * (init_g[1:2, :] - dst_half[0:1, 128:256])
    vin[REACH, 2:4, :] = dst_lw[...] * LOG2E

    def vec_copy(d):
        return remote(
            vin.at[REACH], vin.at[REACH - d], sent.at[2], came.at[0], {"pts": p + d}
        )

    def row_copy(j):
        return remote(
            yout.at[helper(j)], yin.at[h], sent.at[3], came.at[1], {"help": helper(j)}
        )

    steps = [1, -1, 2, -2, 3, -3]
    for j in range(1, n_help):
        row_copy(j).start()
    for d in steps:
        when_there(d, lambda d=d: vec_copy(d).start())
    yin[h] = yout[h]
    if not FROM_VMEM:
        get_src.wait()
    src_half = half_norms(xs[h])

    with jax.named_scope("relay"):
        arrive(xs.at[0, parts[0]], x_recv.at[0])
        x_on(0).start()
        arrive(xs.at[0, parts[0]], x_recv.at[1])
        x_on(1).start()
        for q in range(2):
            for way, d in enumerate((-2, 2)):

                @pl.when(there(d))
                def _(way=way, d=d, q=q):
                    arrive(ys.at[0, parts[0]], y_recv.at[2 * way + q])

                    @pl.when((2 * side == d) & there(-side))
                    def _():
                        y_over(q).start()

                    y_on(way, q).start()

        arrive(xs.at[0], x_recv.at[2])
        arrive(ys.at[0], y_recv.at[4])

    def tiles(k, rows):
        for r in rows:
            inner = lax.dot_general(
                xs[r], ys[k], (((1,), (1,)), ((), ())), preferred_element_type=F32
            )
            inner = inner * SCALE
            for j in range(2):
                for q in range(2):
                    dots[2 * k + j, 2 * r + q] = inner[half * q : half * q + half, 128 * j : 128 * j + 128]

    soon = [h, helper(1), helper(n_help - 1)]

    def one_first(c, carry):
        tiles(lax.select(c < 2, REACH + c * side, REACH + 10 - 4 * c), soon)
        return carry

    def one_later(c, carry):
        d = lax.select(c < 2, side - 2 + 4 * c, -3 * side)
        k = REACH + d

        @pl.when(there(d))
        def _():
            arrive(ys.at[0], y_recv.at[5 + c])

        tiles(k, soon)
        return carry

    with jax.named_scope("tiles1"):
        lax.fori_loop(0, 4, one_first, 0)
    with jax.named_scope("tiles2"):
        lax.fori_loop(0, 3, one_later, 0)
    with jax.named_scope("xlast"):
        arrive(xs.at[0], x_recv.at[3])
    with jax.named_scope("tiles3"):
        for k in range(SPOTS):
            tiles(k, [helper(2)])

    with jax.named_scope("vec"):
        arrive(yin.at[0 : n_help - 1], came.at[1])
        by_count(nears, 2 * REACH, lambda c: arrive(vin.at[0:c], came.at[0]))
    for k in range(SPOTS):
        bvec[k] = vin[k, 0:2, :]

    def fold(parts):
        top = tree(jnp.maximum, parts)
        return top + log2(tree(jnp.add, [jnp.exp2(v - top) for v in parts]))

    def f_copy(it, j, r):
        return remote(
            lsend.at[it, r],
            lrecv.at[it, r, j - 1],
            sent.at[4],
            f_recv.at[it, r],
            {"help": helper(j)},
        )

    lanes = 2 * SPOTS

    def row_sweep(it):
        def mask(r, carry):
            for k in range(SPOTS):
                on = yin[r, k : k + 1, :] > 0.5
                for j in range(2):
                    push[r, 2 * k + j : 2 * k + j + 1, :] = jnp.where(on, bvec[k, j : j + 1, :], NEG)
            return carry

        lax.fori_loop(0, n_help, mask, 0)

        def load(r, n):
            t = [
                dots[c, 2 * r + n // 16, 8 * (n % 16) : 8 * (n % 16) + 8, :]
                + jnp.broadcast_to(push[r, c : c + 1, :], (8, 128))
                for c in range(lanes)
            ]
            return t, tree(jnp.maximum, t)

        def close(r):
            for q in range(2):
                top = peak[2 * r + q].T
                most = jnp.max(top, axis=0, keepdims=True)
                s = total[2 * r + q].T * jnp.exp2(top - most)
                lsend[it, r, q : q + 1, :] = most + log2(jnp.sum(s, axis=0, keepdims=True))

        def send(r):
            for j in (2, 1, 3):
                f_copy(it, j, r).start()

        def one(r, carry):
            before = jnp.maximum(r - 1, 0)
            close(before)
            t, top = load(r, 0)
            for n in range(32):
                later = load(r, n + 1) if n < 31 else None
                at = slice(8 * (n % 16), 8 * (n % 16) + 8)
                peak[2 * r + n // 16, at, :] = top
                total[2 * r + n // 16, at, :] = tree(jnp.add, [jnp.exp2(v - top) for v in t])
                if later:
                    t, top = later
                if n == SEND_AT:

                    @pl.when(r > 0)
                    def _():
                        send(before)

            return carry

        with jax.named_scope("rmain"):
            lax.fori_loop(0, n_help, one, 0)
        with jax.named_scope("rclose"):
            close(n_help - 1)
        send(n_help - 1)

    def column_sweep(it):
        def load(r, n):
            q, c = n // lanes, n % lanes
            u = [
                dots[c, 2 * r + q, 8 * g : 8 * g + 8, :] + lift[q, 8 * g : 8 * g + 8, :]
                for g in range(16)
            ]
            return u, tree(jnp.maximum, u)

        def one(r, carry):
            arrive(lrecv.at[it, r], f_recv.at[it, r])
            force = -fold([lsend[it, r]] + [lrecv[it, r, j] for j in range(n_help - 1)])
            if it == 1:
                flast[r] = force
            force = force + yin[r, 8:10, :]
            for q in range(2):
                lift[q] = jnp.broadcast_to(force[q : q + 1, :], (128, 128)).T
            u, top = load(r, 0)
            for n in range(2 * lanes):
                later = load(r, n + 1) if n + 1 < 2 * lanes else None
                q, c = n // lanes, n % lanes
                cpeak[c, 2 * r + q] = top
                ctotal[c, 2 * r + q] = tree(jnp.add, [jnp.exp2(v - top) for v in u])
                if later:
                    u, top = later
            return carry

        with jax.named_scope("cmain"):
            lax.fori_loop(0, n_help, one, 0)

        def close(k):
            for j in range(2):
                tops = [
                    jnp.where(yin[rh // 2, k : k + 1, :] > 0.5, cpeak[2 * k + j, rh], NEG)
                    for rh in range(2 * n_help)
                ]
                top = tree(jnp.maximum, tops)
                most = jnp.max(top, axis=0, keepdims=True)
                s = tree(
                    jnp.add,
                    [ctotal[2 * k + j, rh] * jnp.exp2(tops[rh] - most) for rh in range(2 * n_help)],
                )
                gsend[it, k, j : j + 1, :] = most + log2(jnp.sum(s, axis=0, keepdims=True))

        with jax.named_scope("cclose"):
            for k in range(SPOTS):
                close(k)

    def g_copy(d):
        low, count = max(0, d), SPOTS - abs(d)
        return remote(
            gsend.at[0, pl.ds(low, count)],
            grecv.at[WIDE - d, pl.ds(low, count)],
            sent.at[6 if d < 0 else 7],
            g_recv.at[1 if d < 0 else 0],
            {"pts": p + d},
        )

    def g_bytes(c):
        most, spots = ((1, 6), (11, 1), (3, 5), (3, 6), (4, 5), (3, 7))[c - 1]
        return grecv.at[0:most, 0:spots]

    def e_copy(d):
        return remote(
            gsend.at[1, d + REACH], glast.at[REACH - d], sent.at[5], came.at[2], {"pts": p + d}
        )

    for it in range(2):
        with jax.named_scope('rows'):
            row_sweep(it)
        with jax.named_scope('cols'):
            column_sweep(it)
        if it == 1:
            pot = flast[h] * (1.0 / SCALE)
            out[0:1, :] = pot[0:1, :] + src_half[0:1, 0:128]
            out[1:2, :] = pot[1:2, :] + src_half[0:1, 128:256]
        if it == 0:
            for d in sorted(wide, key=lambda d: -abs(d)):
                when_there(d, lambda d=d: g_copy(d).start())
            grecv[WIDE] = gsend[0]
            with jax.named_scope('gwait'):
                by_count(lefts, WIDE, lambda c: arrive(g_bytes(c), g_recv.at[0]))
                by_count(rights, WIDE, lambda c: arrive(g_bytes(c), g_recv.at[1]))
            for k in range(SPOTS):
                got = [grecv[k + REACH + e, REACH - e] for e in range(-REACH, REACH + 1)]
                bvec[k] = vin[k, 2:4, :] - fold(got)
        else:
            for d in sorted(near, key=lambda d: -abs(d)):
                when_there(d, lambda d=d: e_copy(d).start())
            glast[REACH] = gsend[1, REACH]
            with jax.named_scope('ewait'):
                by_count(nears, 2 * REACH, lambda c: arrive(glast.at[0:c], came.at[2]))
            pot = -fold([glast[k] for k in range(SPOTS)]) * (1.0 / SCALE)
            out[2:3, :] = pot[0:1, :] + dst_half[0:1, 0:128]
            out[3:4, :] = pot[1:2, :] + dst_half[0:1, 128:256]

    def one_if(d):
        return there(d).astype(jnp.int32)

    blocks = 1 + 2 * one_if(2) + 2 * one_if(-2) + (there(2 * side) & there(-side)).astype(jnp.int32)
    leave(xs.at[0 : n_help - 1], sent.at[0])
    by_count(blocks, 6, lambda c: leave(ys.at[0:c], sent.at[1]))
    by_count(nears, 2 * REACH, lambda c: leave(vin.at[0:c], sent.at[2]))
    leave(yin.at[0 : n_help - 1], sent.at[3])
    leave(lrecv, sent.at[4])
    by_count(nears, 2 * REACH, lambda c: leave(glast.at[0:c], sent.at[5]))
    by_count(lefts, WIDE, lambda c: leave(g_bytes(c), sent.at[6]))
    by_count(rights, WIDE, lambda c: leave(g_bytes(c), sent.at[7]))


def solution(mesh):
    n_pts, n_help = mesh.shape["pts"], mesh.shape["help"]

    def on_device(src_points, dst_points, src_logw, dst_logw, init_g, pair_lists, pair_counts):
        dim = src_points.shape[1]
        vmem = pl.BlockSpec(memory_space=pltpu.VMEM)
        dma = pltpu.SemaphoreType.DMA
        bf16 = jnp.bfloat16
        raw = pl.pallas_call(
            functools.partial(kernel, n_pts, n_help),
            out_shape=jax.ShapeDtypeStruct((4, 128), F32),
            in_specs=[
                pl.BlockSpec(memory_space=pltpu.HBM),
            ]
            * 7,
            out_specs=vmem,
            scratch_shapes=[
                pltpu.VMEM((3, 2, 128), F32),
                pltpu.VMEM(pair_lists.shape, jnp.int32),
                pltpu.SMEM((1,), jnp.int32),
                pltpu.VMEM((n_help, BLOCK, dim), bf16),
                pltpu.VMEM((SPOTS, BLOCK, dim), bf16),
                pltpu.VMEM((SPOTS, 4, 128), F32),
                pltpu.VMEM((n_help, 16, 128), F32),
                pltpu.VMEM((n_help, 16, 128), F32),
                pltpu.VMEM((2 * SPOTS, 2 * n_help, 128, 128), F32),
                pltpu.VMEM((2 * n_help, 128, 128), F32),
                pltpu.VMEM((2 * n_help, 128, 128), F32),
                pltpu.VMEM((2 * SPOTS, 2 * n_help, 8, 128), F32),
                pltpu.VMEM((2 * SPOTS, 2 * n_help, 8, 128), F32),
                pltpu.VMEM((n_help, 2 * SPOTS, 128), F32),
                pltpu.VMEM((2, 128, 128), F32),
                pltpu.VMEM((SPOTS, 2, 128), F32),
                pltpu.VMEM((n_help, 2, 128), F32),
                pltpu.VMEM((2, n_help, 2, 128), F32),
                pltpu.VMEM((2, n_help, n_help - 1, 2, 128), F32),
                pltpu.VMEM((2, SPOTS, 2, 128), F32),
                pltpu.VMEM((2 * WIDE + 1, SPOTS, 2, 128), F32),
                pltpu.VMEM((SPOTS, 2, 128), F32),
                dma((5,)),
                dma((8,)),
                dma((4,)),
                dma((8,)),
                dma((2, n_help)),
                dma((2,)),
                dma((3,)),
            ],
            compiler_params=pltpu.CompilerParams(collective_id=0, has_side_effects=True, vmem_limit_bytes=24 << 20),
            name="sinkhorn",
        )(
            *(pltpu.with_memory_space_constraint(v, pltpu.HBM) for v in (src_points, dst_points, src_logw.reshape(2, 128), dst_logw.reshape(2, 128), init_g.reshape(2, 128), pair_lists)), pair_counts,
        )
        return raw[0:2].reshape(-1), raw[2:4].reshape(-1)

    rows = P(("pts", "help"))
    blocks = P(("pts", "help"), None)
    return jax.shard_map(
        on_device,
        mesh=mesh,
        in_specs=(blocks, blocks, rows, rows, rows, blocks, rows),
        out_specs=(rows, rows),
        check_vma=False,
    )
```

```python
import functools
import math

import jax
import jax.numpy as jnp
from jax import lax
from jax.experimental import pallas as pl
from jax.experimental.pallas import tpu as pltpu
from jax.sharding import PartitionSpec as P

REACH = 3
WIDE = 2 * REACH
SPOTS = 2 * REACH + 1
BLOCK = 256
LOG2E = 1.0 / math.log(2.0)
SCALE = 4.0 * LOG2E
NEG = -1e30
FROM_VMEM = True
SEND_AT = 15
CLOSE_AT = 17
LATE_LATER = True
MESH = pl.DeviceIdType.MESH
F32 = jnp.float32


def tree(op, values):
    values = list(values)
    while len(values) > 1:
        paired = [op(a, b) for a, b in zip(values[::2], values[1::2])]
        values = paired + values[len(paired) * 2 :]
    return values[0]


def log2(x):
    return jnp.log(x) * LOG2E


def half_norms(points):
    wide = points.astype(F32)
    square = wide * wide
    high = square.astype(jnp.bfloat16)
    low = (square - high.astype(F32)).astype(jnp.bfloat16)
    ones = jnp.ones((8, points.shape[1]), jnp.bfloat16)
    dims = (((1,), (1,)), ((), ()))
    total = lax.dot_general(ones, high, dims, preferred_element_type=F32)
    total += lax.dot_general(ones, low, dims, preferred_element_type=F32)
    return 0.5 * total


def kernel(
    n_pts,
    n_help,
    src_hbm,
    dst_hbm,
    src_lw_hbm,
    dst_lw_hbm,
    init_g_hbm,
    lists_hbm,
    counts_hbm,
    out,
    vals,
    lists,
    counts,
    xs,
    ys,
    vin,
    yout,
    yin,
    dots,
    peak,
    total,
    cpeak,
    ctotal,
    push,
    lift,
    bvec,
    flast,
    lsend,
    lrecv,
    gsend,
    grecv,
    glast,
    local_sem,
    sent,
    x_recv,
    y_recv,
    f_recv,
    g_recv,
    came,
):
    p = lax.axis_index("pts")
    h = lax.axis_index("help")
    near = [d for d in range(-REACH, REACH + 1) if d]
    wide = [d for d in range(-WIDE, WIDE + 1) if d]

    def there(d):
        return (p + d >= 0) & (p + d < n_pts)

    def when_there(d, do):
        @pl.when(there(d))
        def _():
            do()

    def helper(j):
        return lax.rem(h + j, n_help)

    def remote(src, dst, send, recv, device):
        return pltpu.make_async_remote_copy(
            src_ref=src,
            dst_ref=dst,
            send_sem=send,
            recv_sem=recv,
            device_id=device,
            device_id_type=MESH,
        )

    side = 1 - 2 * lax.rem(p, 2)

    barrier = pltpu.get_barrier_semaphore()
    for j in range(1, n_help):
        pl.semaphore_signal(barrier, inc=1, device_id={"help": helper(j)}, device_id_type=MESH)
    for d in near:
        when_there(
            d,
            lambda d=d: pl.semaphore_signal(
                barrier, inc=1, device_id={"pts": p + d}, device_id_type=MESH
            ),
        )

    get_dst = pltpu.make_async_copy(dst_hbm, ys.at[REACH], local_sem.at[0])
    get_src = pltpu.make_async_copy(src_hbm, xs.at[h], local_sem.at[4])
    get_vals = [
        pltpu.make_async_copy(a, vals.at[n], local_sem.at[3])
        for n, a in enumerate([dst_lw_hbm, init_g_hbm, src_lw_hbm])
    ]
    get_lists = pltpu.make_async_copy(lists_hbm, lists, local_sem.at[1])
    get_counts = pltpu.make_async_copy(counts_hbm, counts, local_sem.at[2])
    for get in [get_dst, get_src, get_lists, get_counts, *get_vals]:
        get.start()

    with jax.named_scope("barrier"):
        pl.semaphore_wait(
            barrier,
            n_help - 1 + jnp.minimum(p, REACH) + jnp.minimum(n_pts - 1 - p, REACH),
        )

    half = BLOCK // 2
    parts = [pl.ds(0, half), pl.ds(half, half)]

    ahead, behind = {"help": helper(1)}, {"help": helper(n_help - 1)}

    own_x, own_y = (xs.at[h], ys.at[REACH]) if FROM_VMEM else (src_hbm, dst_hbm)

    quarter = half // 2

    def x_own(way, q):
        rows = pl.ds(half * way + quarter * q, quarter) if q < 2 else parts[1 - way]
        return remote(
            own_x.at[rows],
            xs.at[h, rows],
            sent.at[0],
            x_recv.at[2 * way + q if q < 2 else 4],
            (ahead, behind)[way],
        )

    def x_on(way, q):
        r = helper(n_help - 1 if way == 0 else 1)
        here = xs.at[r, pl.ds(half * way + quarter * q, quarter)]
        return remote(here, here, sent.at[0], x_recv.at[5], (ahead, behind)[way])

    def y_own(d, q):
        return remote(
            own_y.at[parts[q]],
            ys.at[REACH - d, parts[q]],
            sent.at[1],
            y_recv.at[lax.div(2 - d, 2) + q],
            {"pts": p + d},
        )

    def y_side():
        return remote(own_y, ys.at[REACH - side], sent.at[1], y_recv.at[4], {"pts": p + side})

    def y_on(d, q):
        return remote(
            ys.at[REACH + d, parts[q]],
            ys.at[REACH + d - side, parts[q]],
            sent.at[1],
            y_recv.at[5 + lax.div(d + 2, 4)],
            {"pts": p + side},
        )

    def y_over(q):
        return remote(
            ys.at[REACH + 2 * side, parts[q]],
            ys.at[REACH + 3 * side, parts[q]],
            sent.at[1],
            y_recv.at[7],
            {"pts": p - side},
        )

    def arrive(ref, sem):
        remote(ref, ref, sent.at[0], sem, ahead).wait_recv()

    def leave(ref, sem):
        remote(ref, ref, sem, x_recv.at[0], ahead).wait_send()

    def by_count(count, most, do):
        for c in range(1, most + 1):
            pl.when(count == c)(lambda c=c: do(c))

    lefts, rights = jnp.minimum(p, WIDE), jnp.minimum(n_pts - 1 - p, WIDE)
    nears = jnp.minimum(p, REACH) + jnp.minimum(n_pts - 1 - p, REACH)

    if FROM_VMEM:
        get_dst.wait()
        get_src.wait()
    early, late = -2 * side, 2 * side
    for q in range(2):
        x_own(0, q).start()
        x_own(1, q).start()
        when_there(early, lambda q=q: y_own(early, q).start())
    y_side().start()
    x_own(0, 2).start()
    x_own(1, 2).start()
    if not LATE_LATER:
        for q in range(2):
            when_there(late, lambda q=q: y_own(late, q).start())

    for d in near:

        @pl.when(jnp.logical_not(there(d)))
        def _():
            ys[d + REACH] = jnp.zeros(ys.shape[1:], ys.dtype)
            vin[d + REACH] = jnp.zeros(vin.shape[1:], F32)
            glast[d + REACH] = jnp.full(glast.shape[1:], NEG, F32)

    for d in wide:

        @pl.when(jnp.logical_not(there(d)))
        def _():
            grecv[d + WIDE] = jnp.full(grecv.shape[1:], NEG, F32)

    for get in [get_lists, get_counts]:
        get.wait()
    remote(vals, vals, local_sem.at[3], x_recv.at[0], ahead).wait_send()
    dst_lw, init_g, src_lw = vals.at[0], vals.at[1], vals.at[2]
    listed = lists[...]
    width = listed.shape[1]
    slot = lax.broadcasted_iota(jnp.int32, (8, width), 1)
    spot = lax.broadcasted_iota(jnp.int32, (8, width), 0)
    live = slot < counts[0]
    for c in range(n_help):
        column = (p + spot - REACH) * n_help + c
        hit = jnp.where((listed == column) & live, 1.0, 0.0)
        yout[c, 0:8, :] = jnp.broadcast_to(jnp.max(hit, axis=1, keepdims=True), (8, 128))
        yout[c, 8:16, :] = jnp.broadcast_to(
            jnp.concatenate([src_lw[...] * LOG2E] * 4, axis=0), (8, 128)
        )

    if not FROM_VMEM:
        get_dst.wait()
    dst_half = half_norms(ys[REACH])
    vin[REACH, 0:1, :] = dst_lw[0:1, :] * LOG2E + SCALE * (init_g[0:1, :] - dst_half[0:1, 0:128])
    vin[REACH, 1:2, :] = dst_lw[1:2, :] * LOG2E + SCALE * (init_g[1:2, :] - dst_half[0:1, 128:256])
    vin[REACH, 2:4, :] = dst_lw[...] * LOG2E

    def vec_copy(d):
        return remote(
            vin.at[REACH], vin.at[REACH - d], sent.at[2], came.at[0], {"pts": p + d}
        )

    def row_copy(j):
        return remote(
            yout.at[helper(j)], yin.at[h], sent.at[3], came.at[1], {"help": helper(j)}
        )

    steps = [1, -1, 2, -2, 3, -3]
    for j in range(1, n_help):
        row_copy(j).start()
    for d in steps:
        when_there(d, lambda d=d: vec_copy(d).start())
    if LATE_LATER:
        for q in range(2):
            when_there(late, lambda q=q: y_own(late, q).start())
    yin[h] = yout[h]
    if not FROM_VMEM:
        get_src.wait()
    src_half = half_norms(xs[h])

    with jax.named_scope("relay"):
        def pass_x(q):
            for way in range(2):
                arrive(xs.at[0, pl.ds(0, quarter)], x_recv.at[2 * way + q])
                x_on(way, q).start()

        def pass_y(d, q, over):
            @pl.when(there(d))
            def _():
                arrive(ys.at[0, parts[0]], y_recv.at[lax.div(d + 2, 2) + q])
                if over:
                    when_there(-side, lambda: y_over(q).start())
                y_on(d, q).start()

        pass_x(0)
        pass_x(1)
        pass_y(2 * side, 0, True)
        pass_y(2 * side, 1, True)
        pass_y(-2 * side, 0, False)
        pass_y(-2 * side, 1, False)
        arrive(xs.at[0], x_recv.at[4])
        arrive(ys.at[0], y_recv.at[4])

    def tiles(k, rows):
        for r in rows:
            inner = lax.dot_general(
                xs[r], ys[k], (((1,), (1,)), ((), ())), preferred_element_type=F32
            )
            inner = inner * SCALE
            for j in range(2):
                for q in range(2):
                    dots[2 * k + j, 2 * r + q] = inner[half * q : half * q + half, 128 * j : 128 * j + 128]

    soon = [h, helper(1), helper(n_help - 1)]

    def one_first(c, carry):
        tiles(lax.select(c < 2, REACH + c * side, REACH + 10 - 4 * c), soon)
        return carry

    def one_later(c, carry):
        d = lax.select(c < 2, side - 2 + 4 * c, -3 * side)
        k = REACH + d

        @pl.when(there(d))
        def _():
            arrive(ys.at[0], y_recv.at[5 + c])

        tiles(k, soon)
        return carry

    with jax.named_scope("tiles1"):
        lax.fori_loop(0, 4, one_first, 0)
    def from_opposite():
        arrive(xs.at[0], x_recv.at[5])

    @pl.when(side > 0)
    def _():
        lax.fori_loop(0, 3, one_later, 0)
        from_opposite()
        for k in range(SPOTS):
            tiles(k, [helper(2)])

    @pl.when(side < 0)
    def _():
        lax.fori_loop(0, 2, one_later, 0)
        from_opposite()
        for k in range(SPOTS - 1):
            tiles(k, [helper(2)])
        when_there(REACH, lambda: arrive(ys.at[0], y_recv.at[7]))
        tiles(SPOTS - 1, [*soon, helper(2)])

    with jax.named_scope("vec"):
        arrive(yin.at[0 : n_help - 1], came.at[1])
        by_count(nears, 2 * REACH, lambda c: arrive(vin.at[0:c], came.at[0]))
    for k in range(SPOTS):
        bvec[k] = vin[k, 0:2, :]

    def fold(parts):
        top = tree(jnp.maximum, parts)
        return top + log2(tree(jnp.add, [jnp.exp2(v - top) for v in parts]))

    def g_copy(d):
        low, count = max(0, d), SPOTS - abs(d)
        return remote(
            gsend.at[0, pl.ds(low, count)],
            grecv.at[WIDE - d, pl.ds(low, count)],
            sent.at[6 if d < 0 else 7],
            g_recv.at[1 if d < 0 else 0],
            {"pts": p + d},
        )

    def g_bytes(c):
        most, spots = ((1, 6), (11, 1), (3, 5), (3, 6), (4, 5), (3, 7))[c - 1]
        return grecv.at[0:most, 0:spots]

    def e_copy(d):
        return remote(
            gsend.at[1, d + REACH], glast.at[REACH - d], sent.at[5], came.at[2], {"pts": p + d}
        )

    rows_of = 2 * n_help

    def f_copy(it, j, r):
        return remote(
            lsend.at[it, r],
            lrecv.at[it, r, j - 1],
            sent.at[4],
            f_recv.at[it, r],
            {"help": helper(j)},
        )

    lanes = 2 * SPOTS

    def row_sweep(it):
        def mask(r, carry):
            for k in range(SPOTS):
                on = yin[r, k : k + 1, :] > 0.5
                for j in range(2):
                    push[r, 2 * k + j : 2 * k + j + 1, :] = jnp.where(on, bvec[k, j : j + 1, :], NEG)
            return carry

        lax.fori_loop(0, n_help, mask, 0)

        def load(r, n):
            t = [
                dots[c, 2 * r + n // 16, 8 * (n % 16) : 8 * (n % 16) + 8, :]
                + jnp.broadcast_to(push[r, c : c + 1, :], (8, 128))
                for c in range(lanes)
            ]
            return t, tree(jnp.maximum, t)

        def close(r, q):
            top = peak[2 * r + q].T
            most = jnp.max(top, axis=0, keepdims=True)
            s = total[2 * r + q].T * jnp.exp2(top - most)
            lsend[it, r, q : q + 1, :] = most + log2(jnp.sum(s, axis=0, keepdims=True))

        def send(r):
            for j in (2, 1, 3):
                f_copy(it, j, r).start()

        def one(r, carry):
            before = jnp.maximum(r - 1, 0)
            close(before, 1)
            t, top = load(r, 0)
            for n in range(32):
                later = load(r, n + 1) if n < 31 else None
                at = slice(8 * (n % 16), 8 * (n % 16) + 8)
                peak[2 * r + n // 16, at, :] = top
                total[2 * r + n // 16, at, :] = tree(jnp.add, [jnp.exp2(v - top) for v in t])
                if later:
                    t, top = later
                if n == SEND_AT:

                    @pl.when(r > 0)
                    def _():
                        send(before)

                if n == CLOSE_AT:
                    close(r, 0)

            return carry

        with jax.named_scope("rmain"):
            lax.fori_loop(0, n_help, one, 0)
        with jax.named_scope("rclose"):
            close(n_help - 1, 1)
        send(n_help - 1)

    def column_sweep(it):
        def begin(r):
            arrive(lrecv.at[it, r], f_recv.at[it, r])
            force = -fold([lsend[it, r]] + [lrecv[it, r, j] for j in range(n_help - 1)])
            if it == 1:
                flast[r] = force
            force = force + yin[r, 8:10, :]
            for q in range(2):
                lift[q] = jnp.broadcast_to(force[q : q + 1, :], (128, 128)).T

        def chunks(r, columns):
            def load(q, c):
                u = [
                    dots[c, 2 * r + q, 8 * g : 8 * g + 8, :] + lift[q, 8 * g : 8 * g + 8, :]
                    for g in range(16)
                ]
                return u, tree(jnp.maximum, u)

            order = [(q, c) for q in range(2) for c in columns]
            u, top = load(*order[0])
            for (q, c), following in zip(order, [*order[1:], None]):
                later = None if following is None else load(*following)
                cpeak[c, 2 * r + q] = top
                ctotal[c, 2 * r + q] = tree(jnp.add, [jnp.exp2(v - top) for v in u])
                if later:
                    u, top = later

        def close(k):
            for j in range(2):
                tops = [
                    jnp.where(yin[rh // 2, k : k + 1, :] > 0.5, cpeak[2 * k + j, rh], NEG)
                    for rh in range(rows_of)
                ]
                top = tree(jnp.maximum, tops)
                most = jnp.max(top, axis=0, keepdims=True)
                s = tree(
                    jnp.add,
                    [ctotal[2 * k + j, rh] * jnp.exp2(tops[rh] - most) for rh in range(rows_of)],
                )
                gsend[it, k, j : j + 1, :] = most + log2(jnp.sum(s, axis=0, keepdims=True))

        def one(r, carry):
            begin(r)
            chunks(r, range(lanes))
            return carry

        with jax.named_scope("cmain"):
            lax.fori_loop(0, n_help - 1, one, 0)
        begin(n_help - 1)
        far = WIDE if it == 0 else REACH
        for spots, reaches in (
            ((6, 0), (far,)),
            ((5, 1), (far - 1,)),
            ((4, 2, 3), range(far - 2, 0, -1)),
        ):
            chunks(n_help - 1, [2 * k + j for k in spots for j in range(2)])
            for k in spots:
                close(k)
            for d in reaches:
                for way in (d, -d):
                    when_there(way, lambda d=way: (e_copy if it else g_copy)(d).start())

    for it in range(2):
        with jax.named_scope('rows'):
            row_sweep(it)
        with jax.named_scope('cols'):
            column_sweep(it)
        if it == 1:
            pot = flast[h] * (1.0 / SCALE)
            out[0:1, :] = pot[0:1, :] + src_half[0:1, 0:128]
            out[1:2, :] = pot[1:2, :] + src_half[0:1, 128:256]
        if it == 0:
            grecv[WIDE] = gsend[0]
            with jax.named_scope('gwait'):
                by_count(lefts, WIDE, lambda c: arrive(g_bytes(c), g_recv.at[0]))
                by_count(rights, WIDE, lambda c: arrive(g_bytes(c), g_recv.at[1]))
            for k in range(SPOTS):
                got = [grecv[k + REACH + e, REACH - e] for e in range(-REACH, REACH + 1)]
                bvec[k] = vin[k, 2:4, :] - fold(got)
        else:
            glast[REACH] = gsend[1, REACH]
            with jax.named_scope('ewait'):
                by_count(nears, 2 * REACH, lambda c: arrive(glast.at[0:c], came.at[2]))
            pot = -fold([glast[k] for k in range(SPOTS)]) * (1.0 / SCALE)
            out[2:3, :] = pot[0:1, :] + dst_half[0:1, 0:128]
            out[3:4, :] = pot[1:2, :] + dst_half[0:1, 128:256]

    def one_if(d):
        return there(d).astype(jnp.int32)

    blocks = 1 + 2 * one_if(2) + 2 * one_if(-2) + (there(2 * side) & there(-side)).astype(jnp.int32)
    leave(xs.at[0 : n_help - 1], sent.at[0])
    by_count(blocks, 6, lambda c: leave(ys.at[0:c], sent.at[1]))
    by_count(nears, 2 * REACH, lambda c: leave(vin.at[0:c], sent.at[2]))
    leave(yin.at[0 : n_help - 1], sent.at[3])
    leave(lrecv, sent.at[4])
    by_count(nears, 2 * REACH, lambda c: leave(glast.at[0:c], sent.at[5]))
    by_count(lefts, WIDE, lambda c: leave(g_bytes(c), sent.at[6]))
    by_count(rights, WIDE, lambda c: leave(g_bytes(c), sent.at[7]))


def solution(mesh):
    n_pts, n_help = mesh.shape["pts"], mesh.shape["help"]

    def on_device(src_points, dst_points, src_logw, dst_logw, init_g, pair_lists, pair_counts):
        dim = src_points.shape[1]
        vmem = pl.BlockSpec(memory_space=pltpu.VMEM)
        dma = pltpu.SemaphoreType.DMA
        bf16 = jnp.bfloat16
        raw = pl.pallas_call(
            functools.partial(kernel, n_pts, n_help),
            out_shape=jax.ShapeDtypeStruct((4, 128), F32),
            in_specs=[
                pl.BlockSpec(memory_space=pltpu.HBM),
            ]
            * 7,
            out_specs=vmem,
            scratch_shapes=[
                pltpu.VMEM((3, 2, 128), F32),
                pltpu.VMEM(pair_lists.shape, jnp.int32),
                pltpu.SMEM((1,), jnp.int32),
                pltpu.VMEM((n_help, BLOCK, dim), bf16),
                pltpu.VMEM((SPOTS, BLOCK, dim), bf16),
                pltpu.VMEM((SPOTS, 4, 128), F32),
                pltpu.VMEM((n_help, 16, 128), F32),
                pltpu.VMEM((n_help, 16, 128), F32),
                pltpu.VMEM((2 * SPOTS, 2 * n_help, 128, 128), F32),
                pltpu.VMEM((2 * n_help, 128, 128), F32),
                pltpu.VMEM((2 * n_help, 128, 128), F32),
                pltpu.VMEM((2 * SPOTS, 2 * n_help, 8, 128), F32),
                pltpu.VMEM((2 * SPOTS, 2 * n_help, 8, 128), F32),
                pltpu.VMEM((n_help, 2 * SPOTS, 128), F32),
                pltpu.VMEM((2, 128, 128), F32),
                pltpu.VMEM((SPOTS, 2, 128), F32),
                pltpu.VMEM((n_help, 2, 128), F32),
                pltpu.VMEM((2, n_help, 2, 128), F32),
                pltpu.VMEM((2, n_help, n_help - 1, 2, 128), F32),
                pltpu.VMEM((2, SPOTS, 2, 128), F32),
                pltpu.VMEM((2 * WIDE + 1, SPOTS, 2, 128), F32),
                pltpu.VMEM((SPOTS, 2, 128), F32),
                dma((5,)),
                dma((8,)),
                dma((6,)),
                dma((8,)),
                dma((2, n_help)),
                dma((2,)),
                dma((3,)),
            ],
            compiler_params=pltpu.CompilerParams(collective_id=0, has_side_effects=True, vmem_limit_bytes=24 << 20),
            name="sinkhorn",
        )(
            *(pltpu.with_memory_space_constraint(v, pltpu.HBM) for v in (src_points, dst_points, src_logw.reshape(2, 128), dst_logw.reshape(2, 128), init_g.reshape(2, 128), pair_lists)), pair_counts,
        )
        return raw[0:2].reshape(-1), raw[2:4].reshape(-1)

    rows = P(("pts", "help"))
    blocks = P(("pts", "help"), None)
    return jax.shard_map(
        on_device,
        mesh=mesh,
        in_specs=(blocks, blocks, rows, rows, rows, blocks, rows),
        out_specs=(rows, rows),
        check_vma=False,
    )
```

```python
import functools
import math

import jax
import jax.numpy as jnp
from jax import lax
from jax.experimental import pallas as pl
from jax.experimental.pallas import tpu as pltpu
from jax.sharding import PartitionSpec as P

REACH = 3
WIDE = 2 * REACH
SPOTS = 2 * REACH + 1
BLOCK = 256
LOG2E = 1.0 / math.log(2.0)
SCALE = 4.0 * LOG2E
NEG = -1e30
FROM_VMEM = True
SEND_AT = 15
CLOSE_AT = 17
LATE_LATER = True
MESH = pl.DeviceIdType.MESH
F32 = jnp.float32


def tree(op, values):
    values = list(values)
    while len(values) > 1:
        paired = [op(a, b) for a, b in zip(values[::2], values[1::2])]
        values = paired + values[len(paired) * 2 :]
    return values[0]


def log2(x):
    return jnp.log(x) * LOG2E


def half_norms(points):
    wide = points.astype(F32)
    square = wide * wide
    high = square.astype(jnp.bfloat16)
    low = (square - high.astype(F32)).astype(jnp.bfloat16)
    ones = jnp.ones((8, points.shape[1]), jnp.bfloat16)
    dims = (((1,), (1,)), ((), ()))
    total = lax.dot_general(ones, high, dims, preferred_element_type=F32)
    total += lax.dot_general(ones, low, dims, preferred_element_type=F32)
    return 0.5 * total


def kernel(
    n_pts,
    n_help,
    src_hbm,
    dst_hbm,
    src_lw_hbm,
    dst_lw_hbm,
    init_g_hbm,
    lists_hbm,
    counts_hbm,
    out,
    vals,
    lists,
    counts,
    xs,
    ys,
    vin,
    yout,
    yin,
    dots,
    peak,
    total,
    cpeak,
    ctotal,
    push,
    lift,
    bvec,
    flast,
    lsend,
    lrecv,
    gsend,
    grecv,
    glast,
    local_sem,
    sent,
    x_recv,
    y_recv,
    f_recv,
    g_recv,
    came,
):
    p = lax.axis_index("pts")
    h = lax.axis_index("help")
    near = [d for d in range(-REACH, REACH + 1) if d]
    wide = [d for d in range(-WIDE, WIDE + 1) if d]

    def there(d):
        return (p + d >= 0) & (p + d < n_pts)

    def when_there(d, do):
        @pl.when(there(d))
        def _():
            do()

    def helper(j):
        return lax.rem(h + j, n_help)

    def remote(src, dst, send, recv, device):
        return pltpu.make_async_remote_copy(
            src_ref=src,
            dst_ref=dst,
            send_sem=send,
            recv_sem=recv,
            device_id=device,
            device_id_type=MESH,
        )

    side = 1 - 2 * lax.rem(p, 2)

    barrier = pltpu.get_barrier_semaphore()
    for j in range(1, n_help):
        pl.semaphore_signal(barrier, inc=1, device_id={"help": helper(j)}, device_id_type=MESH)
    for d in near:
        when_there(
            d,
            lambda d=d: pl.semaphore_signal(
                barrier, inc=1, device_id={"pts": p + d}, device_id_type=MESH
            ),
        )

    get_dst = pltpu.make_async_copy(dst_hbm, ys.at[REACH], local_sem.at[0])
    get_src = pltpu.make_async_copy(src_hbm, xs.at[h], local_sem.at[4])
    get_vals = [
        pltpu.make_async_copy(a, vals.at[n], local_sem.at[3])
        for n, a in enumerate([dst_lw_hbm, init_g_hbm, src_lw_hbm])
    ]
    get_lists = pltpu.make_async_copy(lists_hbm, lists, local_sem.at[1])
    get_counts = pltpu.make_async_copy(counts_hbm, counts, local_sem.at[2])
    for get in [get_dst, get_src, get_lists, get_counts, *get_vals]:
        get.start()

    with jax.named_scope("barrier"):
        pl.semaphore_wait(
            barrier,
            n_help - 1 + jnp.minimum(p, REACH) + jnp.minimum(n_pts - 1 - p, REACH),
        )

    half = BLOCK // 2
    parts = [pl.ds(0, half), pl.ds(half, half)]

    ahead, behind = {"help": helper(1)}, {"help": helper(n_help - 1)}

    own_x, own_y = (xs.at[h], ys.at[REACH]) if FROM_VMEM else (src_hbm, dst_hbm)

    quarter = half // 2

    def x_own(way, q):
        rows = pl.ds(half * way + quarter * q, quarter) if q < 2 else parts[1 - way]
        return remote(
            own_x.at[rows],
            xs.at[h, rows],
            sent.at[0],
            x_recv.at[2 * way + q if q < 2 else 4],
            (ahead, behind)[way],
        )

    def x_on(way, q):
        r = helper(n_help - 1 if way == 0 else 1)
        here = xs.at[r, pl.ds(half * way + quarter * q, quarter)]
        return remote(here, here, sent.at[0], x_recv.at[5], (ahead, behind)[way])

    def y_own(d, q):
        return remote(
            own_y.at[parts[q]],
            ys.at[REACH - d, parts[q]],
            sent.at[1],
            y_recv.at[lax.div(2 - d, 2) + q],
            {"pts": p + d},
        )

    def y_side():
        return remote(own_y, ys.at[REACH - side], sent.at[1], y_recv.at[4], {"pts": p + side})

    def y_on(d, q):
        return remote(
            ys.at[REACH + d, parts[q]],
            ys.at[REACH + d - side, parts[q]],
            sent.at[1],
            y_recv.at[5 + lax.div(d + 2, 4)],
            {"pts": p + side},
        )

    def y_over(q):
        return remote(
            ys.at[REACH + 2 * side, parts[q]],
            ys.at[REACH + 3 * side, parts[q]],
            sent.at[1],
            y_recv.at[7],
            {"pts": p - side},
        )

    def arrive(ref, sem):
        remote(ref, ref, sent.at[0], sem, ahead).wait_recv()

    def leave(ref, sem):
        remote(ref, ref, sem, x_recv.at[0], ahead).wait_send()

    def by_count(count, most, do):
        for c in range(1, most + 1):
            pl.when(count == c)(lambda c=c: do(c))

    lefts, rights = jnp.minimum(p, WIDE), jnp.minimum(n_pts - 1 - p, WIDE)
    nears = jnp.minimum(p, REACH) + jnp.minimum(n_pts - 1 - p, REACH)

    if FROM_VMEM:
        get_dst.wait()
        get_src.wait()
    early, late = -2 * side, 2 * side
    for q in range(2):
        x_own(0, q).start()
        x_own(1, q).start()
        when_there(early, lambda q=q: y_own(early, q).start())
    y_side().start()
    x_own(0, 2).start()
    x_own(1, 2).start()
    if not LATE_LATER:
        for q in range(2):
            when_there(late, lambda q=q: y_own(late, q).start())

    for d in near:

        @pl.when(jnp.logical_not(there(d)))
        def _():
            ys[d + REACH] = jnp.zeros(ys.shape[1:], ys.dtype)
            vin[d + REACH] = jnp.zeros(vin.shape[1:], F32)
            glast[d + REACH] = jnp.full(glast.shape[1:], NEG, F32)

    for d in wide:

        @pl.when(jnp.logical_not(there(d)))
        def _():
            grecv[d + WIDE] = jnp.full(grecv.shape[1:], NEG, F32)

    for get in [get_lists, get_counts]:
        get.wait()
    remote(vals, vals, local_sem.at[3], x_recv.at[0], ahead).wait_send()
    dst_lw, init_g, src_lw = vals.at[0], vals.at[1], vals.at[2]
    listed = lists[...]
    width = listed.shape[1]
    slot = lax.broadcasted_iota(jnp.int32, (8, width), 1)
    spot = lax.broadcasted_iota(jnp.int32, (8, width), 0)
    live = slot < counts[0]
    for c in range(n_help):
        column = (p + spot - REACH) * n_help + c
        hit = jnp.where((listed == column) & live, 1.0, 0.0)
        yout[c, 0:8, :] = jnp.broadcast_to(jnp.max(hit, axis=1, keepdims=True), (8, 128))
        yout[c, 8:16, :] = jnp.broadcast_to(
            jnp.concatenate([src_lw[...] * LOG2E] * 4, axis=0), (8, 128)
        )

    if not FROM_VMEM:
        get_dst.wait()
    dst_half = half_norms(ys[REACH])
    vin[REACH, 0:1, :] = dst_lw[0:1, :] * LOG2E + SCALE * (init_g[0:1, :] - dst_half[0:1, 0:128])
    vin[REACH, 1:2, :] = dst_lw[1:2, :] * LOG2E + SCALE * (init_g[1:2, :] - dst_half[0:1, 128:256])
    vin[REACH, 2:4, :] = dst_lw[...] * LOG2E

    def vec_copy(d):
        return remote(
            vin.at[REACH], vin.at[REACH - d], sent.at[2], came.at[0], {"pts": p + d}
        )

    def row_copy(j):
        return remote(
            yout.at[helper(j)], yin.at[h], sent.at[3], came.at[1], {"help": helper(j)}
        )

    steps = [1, -1, 2, -2, 3, -3]
    for j in range(1, n_help):
        row_copy(j).start()
    for d in steps:
        when_there(d, lambda d=d: vec_copy(d).start())
    if LATE_LATER:
        for q in range(2):
            when_there(late, lambda q=q: y_own(late, q).start())
    yin[h] = yout[h]
    if not FROM_VMEM:
        get_src.wait()
    src_half = half_norms(xs[h])

    def tiles(k, rows):
        for r in rows:
            inner = lax.dot_general(
                xs[r], ys[k], (((1,), (1,)), ((), ())), preferred_element_type=F32
            )
            inner = inner * SCALE
            for j in range(2):
                for q in range(2):
                    dots[2 * k + j, 2 * r + q] = inner[half * q : half * q + half, 128 * j : 128 * j + 128]

    tiles(REACH, [h])
    arrive(ys.at[0], y_recv.at[4])
    tiles(REACH + side, [h])

    with jax.named_scope("relay"):
        def pass_x(q):
            for way in range(2):
                arrive(xs.at[0, pl.ds(0, quarter)], x_recv.at[2 * way + q])
                x_on(way, q).start()

        def pass_y(d, q, over):
            @pl.when(there(d))
            def _():
                arrive(ys.at[0, parts[0]], y_recv.at[lax.div(d + 2, 2) + q])
                if over:
                    when_there(-side, lambda: y_over(q).start())
                y_on(d, q).start()

        pass_x(0)
        pass_x(1)
        pass_y(2 * side, 0, True)
        pass_y(2 * side, 1, True)
        pass_y(-2 * side, 0, False)
        pass_y(-2 * side, 1, False)
        arrive(xs.at[0], x_recv.at[4])

    soon = [h, helper(1), helper(n_help - 1)]

    with jax.named_scope("tiles1"):
        for k in (REACH, REACH + side):
            tiles(k, soon[1:])
        for k in (REACH + 2, REACH - 2):
            tiles(k, soon)

    def later(count):
        slots = [(c, d) for c, d in enumerate((side - 2, side + 2, -3 * side))][:count]
        for c, d in slots:
            when_there(d, lambda c=c: arrive(ys.at[0], y_recv.at[5 + c]))
        for c, d in slots:
            tiles(REACH + d, soon)

    def from_opposite():
        arrive(xs.at[0], x_recv.at[5])

    @pl.when(side > 0)
    def _():
        later(3)
        from_opposite()
        for k in range(SPOTS):
            tiles(k, [helper(2)])

    @pl.when(side < 0)
    def _():
        later(2)
        from_opposite()
        for k in range(SPOTS - 1):
            tiles(k, [helper(2)])
        when_there(REACH, lambda: arrive(ys.at[0], y_recv.at[7]))
        tiles(SPOTS - 1, [*soon, helper(2)])

    with jax.named_scope("vec"):
        arrive(yin.at[0 : n_help - 1], came.at[1])
        by_count(nears, 2 * REACH, lambda c: arrive(vin.at[0:c], came.at[0]))
    for k in range(SPOTS):
        bvec[k] = vin[k, 0:2, :]

    def fold(parts):
        top = tree(jnp.maximum, parts)
        return top + log2(tree(jnp.add, [jnp.exp2(v - top) for v in parts]))

    def g_copy(d):
        low, count = max(0, d), SPOTS - abs(d)
        return remote(
            gsend.at[0, pl.ds(low, count)],
            grecv.at[WIDE - d, pl.ds(low, count)],
            sent.at[6 if d < 0 else 7],
            g_recv.at[1 if d < 0 else 0],
            {"pts": p + d},
        )

    def g_bytes(c):
        most, spots = ((1, 6), (11, 1), (3, 5), (3, 6), (4, 5), (3, 7))[c - 1]
        return grecv.at[0:most, 0:spots]

    def e_copy(d):
        return remote(
            gsend.at[1, d + REACH], glast.at[REACH - d], sent.at[5], came.at[2], {"pts": p + d}
        )

    rows_of = 2 * n_help

    def f_copy(it, j, r):
        return remote(
            lsend.at[it, r],
            lrecv.at[it, r, j - 1],
            sent.at[4],
            f_recv.at[it, r],
            {"help": helper(j)},
        )

    lanes = 2 * SPOTS

    def row_sweep(it):
        def mask(r, carry):
            for k in range(SPOTS):
                on = yin[r, k : k + 1, :] > 0.5
                for j in range(2):
                    push[r, 2 * k + j : 2 * k + j + 1, :] = jnp.where(on, bvec[k, j : j + 1, :], NEG)
            return carry

        lax.fori_loop(0, n_help, mask, 0)

        def load(r, n):
            t = [
                dots[c, 2 * r + n // 16, 8 * (n % 16) : 8 * (n % 16) + 8, :]
                + jnp.broadcast_to(push[r, c : c + 1, :], (8, 128))
                for c in range(lanes)
            ]
            return t, tree(jnp.maximum, t)

        def close(r, q):
            top = peak[2 * r + q].T
            most = jnp.max(top, axis=0, keepdims=True)
            s = total[2 * r + q].T * jnp.exp2(top - most)
            lsend[it, r, q : q + 1, :] = most + log2(jnp.sum(s, axis=0, keepdims=True))

        def send(r):
            for j in (2, 1, 3):
                f_copy(it, j, r).start()

        def one(r, carry):
            before = jnp.maximum(r - 1, 0)
            close(before, 1)
            t, top = load(r, 0)
            for n in range(32):
                later = load(r, n + 1) if n < 31 else None
                at = slice(8 * (n % 16), 8 * (n % 16) + 8)
                peak[2 * r + n // 16, at, :] = top
                total[2 * r + n // 16, at, :] = tree(jnp.add, [jnp.exp2(v - top) for v in t])
                if later:
                    t, top = later
                if n == SEND_AT:

                    @pl.when(r > 0)
                    def _():
                        send(before)

                if n == CLOSE_AT:
                    close(r, 0)

            return carry

        with jax.named_scope("rmain"):
            lax.fori_loop(0, n_help, one, 0)
        with jax.named_scope("rclose"):
            close(n_help - 1, 1)
        send(n_help - 1)

    def column_sweep(it):
        def begin(r):
            arrive(lrecv.at[it, r], f_recv.at[it, r])
            force = -fold([lsend[it, r]] + [lrecv[it, r, j] for j in range(n_help - 1)])
            if it == 1:
                flast[r] = force
            force = force + yin[r, 8:10, :]
            for q in range(2):
                lift[q] = jnp.broadcast_to(force[q : q + 1, :], (128, 128)).T

        def chunks(r, columns):
            def load(q, c):
                u = [
                    dots[c, 2 * r + q, 8 * g : 8 * g + 8, :] + lift[q, 8 * g : 8 * g + 8, :]
                    for g in range(16)
                ]
                return u, tree(jnp.maximum, u)

            order = [(q, c) for q in range(2) for c in columns]
            u, top = load(*order[0])
            for (q, c), following in zip(order, [*order[1:], None]):
                later = None if following is None else load(*following)
                cpeak[c, 2 * r + q] = top
                ctotal[c, 2 * r + q] = tree(jnp.add, [jnp.exp2(v - top) for v in u])
                if later:
                    u, top = later

        def close(k):
            for j in range(2):
                tops = [
                    jnp.where(yin[rh // 2, k : k + 1, :] > 0.5, cpeak[2 * k + j, rh], NEG)
                    for rh in range(rows_of)
                ]
                top = tree(jnp.maximum, tops)
                most = jnp.max(top, axis=0, keepdims=True)
                s = tree(
                    jnp.add,
                    [ctotal[2 * k + j, rh] * jnp.exp2(tops[rh] - most) for rh in range(rows_of)],
                )
                gsend[it, k, j : j + 1, :] = most + log2(jnp.sum(s, axis=0, keepdims=True))

        def one(r, carry):
            begin(r)
            chunks(r, range(lanes))
            return carry

        with jax.named_scope("cmain"):
            lax.fori_loop(0, n_help - 1, one, 0)
        begin(n_help - 1)
        far = WIDE if it == 0 else REACH
        for spots, reaches in (
            ((6, 0), (far,)),
            ((5, 1), (far - 1,)),
            ((4, 2, 3), range(far - 2, 0, -1)),
        ):
            chunks(n_help - 1, [2 * k + j for k in spots for j in range(2)])
            for k in spots:
                close(k)
            for d in reaches:
                for way in (d, -d):
                    when_there(way, lambda d=way: (e_copy if it else g_copy)(d).start())

    for it in range(2):
        with jax.named_scope('rows'):
            row_sweep(it)
        with jax.named_scope('cols'):
            column_sweep(it)
        if it == 1:
            pot = flast[h] * (1.0 / SCALE)
            out[0:1, :] = pot[0:1, :] + src_half[0:1, 0:128]
            out[1:2, :] = pot[1:2, :] + src_half[0:1, 128:256]
        if it == 0:
            grecv[WIDE] = gsend[0]
            with jax.named_scope('gwait'):
                by_count(lefts, WIDE, lambda c: arrive(g_bytes(c), g_recv.at[0]))
                by_count(rights, WIDE, lambda c: arrive(g_bytes(c), g_recv.at[1]))
            for k in range(SPOTS):
                got = [grecv[k + REACH + e, REACH - e] for e in range(-REACH, REACH + 1)]
                bvec[k] = vin[k, 2:4, :] - fold(got)
        else:
            glast[REACH] = gsend[1, REACH]
            with jax.named_scope('ewait'):
                by_count(nears, 2 * REACH, lambda c: arrive(glast.at[0:c], came.at[2]))
            pot = -fold([glast[k] for k in range(SPOTS)]) * (1.0 / SCALE)
            out[2:3, :] = pot[0:1, :] + dst_half[0:1, 0:128]
            out[3:4, :] = pot[1:2, :] + dst_half[0:1, 128:256]

    def one_if(d):
        return there(d).astype(jnp.int32)

    blocks = 1 + 2 * one_if(2) + 2 * one_if(-2) + (there(2 * side) & there(-side)).astype(jnp.int32)
    leave(xs.at[0 : n_help - 1], sent.at[0])
    by_count(blocks, 6, lambda c: leave(ys.at[0:c], sent.at[1]))
    by_count(nears, 2 * REACH, lambda c: leave(vin.at[0:c], sent.at[2]))
    leave(yin.at[0 : n_help - 1], sent.at[3])
    leave(lrecv, sent.at[4])
    by_count(nears, 2 * REACH, lambda c: leave(glast.at[0:c], sent.at[5]))
    by_count(lefts, WIDE, lambda c: leave(g_bytes(c), sent.at[6]))
    by_count(rights, WIDE, lambda c: leave(g_bytes(c), sent.at[7]))


def solution(mesh):
    n_pts, n_help = mesh.shape["pts"], mesh.shape["help"]

    def on_device(src_points, dst_points, src_logw, dst_logw, init_g, pair_lists, pair_counts):
        dim = src_points.shape[1]
        vmem = pl.BlockSpec(memory_space=pltpu.VMEM)
        dma = pltpu.SemaphoreType.DMA
        bf16 = jnp.bfloat16
        raw = pl.pallas_call(
            functools.partial(kernel, n_pts, n_help),
            out_shape=jax.ShapeDtypeStruct((4, 128), F32),
            in_specs=[
                pl.BlockSpec(memory_space=pltpu.HBM),
            ]
            * 7,
            out_specs=vmem,
            scratch_shapes=[
                pltpu.VMEM((3, 2, 128), F32),
                pltpu.VMEM(pair_lists.shape, jnp.int32),
                pltpu.SMEM((1,), jnp.int32),
                pltpu.VMEM((n_help, BLOCK, dim), bf16),
                pltpu.VMEM((SPOTS, BLOCK, dim), bf16),
                pltpu.VMEM((SPOTS, 4, 128), F32),
                pltpu.VMEM((n_help, 16, 128), F32),
                pltpu.VMEM((n_help, 16, 128), F32),
                pltpu.VMEM((2 * SPOTS, 2 * n_help, 128, 128), F32),
                pltpu.VMEM((2 * n_help, 128, 128), F32),
                pltpu.VMEM((2 * n_help, 128, 128), F32),
                pltpu.VMEM((2 * SPOTS, 2 * n_help, 8, 128), F32),
                pltpu.VMEM((2 * SPOTS, 2 * n_help, 8, 128), F32),
                pltpu.VMEM((n_help, 2 * SPOTS, 128), F32),
                pltpu.VMEM((2, 128, 128), F32),
                pltpu.VMEM((SPOTS, 2, 128), F32),
                pltpu.VMEM((n_help, 2, 128), F32),
                pltpu.VMEM((2, n_help, 2, 128), F32),
                pltpu.VMEM((2, n_help, n_help - 1, 2, 128), F32),
                pltpu.VMEM((2, SPOTS, 2, 128), F32),
                pltpu.VMEM((2 * WIDE + 1, SPOTS, 2, 128), F32),
                pltpu.VMEM((SPOTS, 2, 128), F32),
                dma((5,)),
                dma((8,)),
                dma((6,)),
                dma((8,)),
                dma((2, n_help)),
                dma((2,)),
                dma((3,)),
            ],
            compiler_params=pltpu.CompilerParams(collective_id=0, has_side_effects=True, vmem_limit_bytes=24 << 20),
            name="sinkhorn",
        )(
            *(pltpu.with_memory_space_constraint(v, pltpu.HBM) for v in (src_points, dst_points, src_logw.reshape(2, 128), dst_logw.reshape(2, 128), init_g.reshape(2, 128), pair_lists)), pair_counts,
        )
        return raw[0:2].reshape(-1), raw[2:4].reshape(-1)

    rows = P(("pts", "help"))
    blocks = P(("pts", "help"), None)
    return jax.shard_map(
        on_device,
        mesh=mesh,
        in_specs=(blocks, blocks, rows, rows, rows, blocks, rows),
        out_specs=(rows, rows),
        check_vma=False,
    )
```
